256 devices in a mesh: narrow: 8 (over y, core), wide: 32 (over z, x).
Axes of the slice: x: 4, y: 4, z: 8, core: 2. Of those that a mesh axis runs over, the one named last changes fastest.
Arguments:
- queries: bfloat16 [262144, 128], P(('wide', 'narrow')), may hold values from -0.5 to 0.5
- keys: bfloat16 [262144, 128], P(('wide', 'narrow')), may hold values from -6 to 6
- values: bfloat16 [262144, 1024], P(('wide', 'narrow')), may hold values from -6 to 6
- log_decay: float32 [8, 262144], P(None, ('wide', 'narrow')), may hold values from -1 to 0
- level_weight: float32 [11, 8, 262144], P(None, None, ('wide', 'narrow')), may hold values from 0 to 2
- norm_gain: float32 [1024], replicated, may hold values from 0.5 to 1.5
Outputs:
- layer_output: bfloat16 [262144, 1024], P(('wide', 'narrow'))
The draws below stay inside these ranges and needn't reach their ends.
All inputs are finite; a program needn't handle non-finite values.
Results may differ from the reference program's by a relative error of at most 0.005.
Values sent between devices are 32-bit elements; how exact they have to be, the bound alone decides.
A program may use at most 128 MiB of HBM per device.

```python
import math
import jax
import jax.numpy as jnp
from jax import lax

HEADS = 8
KEY = 128
HEAD = 128
SPAN = 256
TOK_DEV = 1024
TOKEN_COUNT = 262144
LEVELS = 11


def draw_log_decay(key, part):
    sequence_lanes = jax.random.split(key, 7)
    quick = jax.random.randint(sequence_lanes[0], (HEADS,), 0, 2) == 1
    slow_total = jax.random.uniform(sequence_lanes[1], (HEADS,), jnp.float32, 0.03, 0.3)
    quick_rate = jnp.exp(jax.random.uniform(sequence_lanes[2], (HEADS,), jnp.float32, math.log(1.0 / 50.0), math.log(1.0 / 30.0)))
    token_factor_scale = jnp.exp(jax.random.uniform(sequence_lanes[3], (HEADS, TOKEN_COUNT), jnp.float32, -math.log(2.0), math.log(2.0)))
    block_factor_scale = jnp.exp(jax.random.uniform(sequence_lanes[4], (HEADS, TOKEN_COUNT // TOK_DEV), jnp.float32, -math.log(2.0), math.log(2.0)))
    block_factor_scale = jnp.repeat(block_factor_scale, TOK_DEV, axis=1)
    baseline_rate = jnp.where(quick[:, None], quick_rate[:, None], (slow_total / TOKEN_COUNT)[:, None])
    surge_positions = jax.random.randint(sequence_lanes[5], (3,), 0, TOKEN_COUNT)
    surge_lengths = jax.random.uniform(sequence_lanes[6], (3,), jnp.float32, 0.22, 0.5)
    slot_positions = jnp.arange(TOKEN_COUNT)
    surge_groups = jnp.sum(jnp.where(slot_positions[None, :] == surge_positions[:, None], surge_lengths[:, None], 0.0), axis=0)
    return -(baseline_rate * token_factor_scale * block_factor_scale + surge_groups[None, :])


def draw_level_weight(key, part):
    level_index = jnp.arange(LEVELS, dtype=jnp.float32)[:, None, None]
    base_weight = jnp.exp(jax.random.uniform(key, (LEVELS, HEADS, TOKEN_COUNT), jnp.float32, -math.log(2.0), math.log(2.0)))
    return base_weight * jnp.exp2(-0.5 * level_index)


def shard_levels(stream_key, extent, pieces, low, largest):
    factor_of, own = 1.0, jax.random.fold_in(stream_key, 6)
    for dim, shards_of in pieces:
        draws = jnp.exp(jax.random.uniform(jax.random.fold_in(own, dim), (shards_of,), jnp.float32, low / len(pieces), largest / len(pieces)))
        factor_of = factor_of * jnp.repeat(draws, extent[dim] // shards_of).reshape([-1 if axis == dim else 1 for axis in range(len(extent))])
    return factor_of


def gaussian(rng, dims, scale, bound, cuts=(), kind=jnp.bfloat16):
    values = jax.random.normal(rng, dims, jnp.float32) * scale
    if len(cuts) > 0:
        values = shard_levels(rng, dims, cuts, -0.22, 0.18) * values
    return jnp.clip(values, min=-bound, max=bound).astype(kind)


def setup_inputs(seed: int = 0) -> dict:
    splits = jax.random.split(jax.random.key(seed), 7)
    queries = gaussian(splits[0], (TOKEN_COUNT, KEY), KEY ** -0.5, 0.5, ((0, 256),))
    keys = gaussian(splits[1], (TOKEN_COUNT, KEY), 1.0, 6.0, ((0, 256),))
    values = gaussian(splits[2], (TOKEN_COUNT, HEADS * HEAD), 1.0, 6.0, ((0, 256),))
    log_decay = draw_log_decay(jax.random.fold_in(splits[6], 71), 0)
    level_weight = draw_level_weight(jax.random.fold_in(splits[6], 71), 0)
    norm_gain = jnp.clip(1.0 + 0.1 * jax.random.normal(splits[5], (HEADS * HEAD,), jnp.float32), 0.5, 1.5)
    return {"queries": queries, "keys": keys, "values": values, "log_decay": log_decay, "level_weight": level_weight, "norm_gain": norm_gain}


def reference(queries, keys, values, log_decay, level_weight, norm_gain):
    block_count = TOKEN_COUNT // SPAN
    upper_levels = LEVELS - 1
    query_blocks = queries.reshape(block_count, SPAN, KEY)
    key_blocks = keys.reshape(block_count, SPAN, KEY)
    value_blocks = values.reshape(block_count, SPAN, HEADS, HEAD)
    decay_blocks = log_decay.reshape(HEADS, block_count, SPAN).transpose(1, 0, 2)
    weight_blocks = level_weight.reshape(LEVELS, HEADS, block_count, SPAN).transpose(2, 0, 1, 3)
    positions = jnp.arange(SPAN, dtype=jnp.int32)
    causal = positions[:, None] >= positions[None, :]
    level_ids = jnp.arange(upper_levels, dtype=jnp.int32)
    periods = jnp.left_shift(jnp.ones_like(level_ids), level_ids)
    gain_rows = norm_gain.reshape(HEADS, HEAD)

    def advance(carried, inputs):
        running, finished = carried
        query_rows, key_rows, value_rows, decay_rows, weight_rows, block_id = inputs
        within = jnp.cumsum(decay_rows, axis=1)
        scores = jnp.dot(query_rows, key_rows.T, preferred_element_type=jnp.float32)
        spread = jnp.where(causal[None], within[:, :, None] - within[:, None, :], -1e+30)
        mixing = (scores[None] * jnp.exp(spread) * weight_rows[0][:, :, None]).astype(jnp.bfloat16)
        value_float = value_rows.astype(jnp.float32)
        intra = jnp.einsum('hij,jhp->hip', mixing.astype(jnp.float32), value_float)
        present = jnp.bitwise_and(jnp.right_shift(block_id, level_ids), 1).astype(jnp.float32)
        level_states = (finished * present[:, None, None, None]).astype(jnp.bfloat16)
        projected = jnp.einsum('in,lhnp->lhip', query_rows.astype(jnp.float32), level_states.astype(jnp.float32))
        inter = lax.optimization_barrier(jnp.sum(weight_rows[1:][:, :, :, None] * projected, axis=0))
        mixed = intra + jnp.exp(within)[:, :, None] * inter
        block_total = within[:, -1]
        decayed_keys = (jnp.exp(block_total[:, None] - within)[:, :, None] * key_rows.astype(jnp.float32)[None]).astype(jnp.bfloat16)
        state = jnp.einsum('hjn,jhp->hnp', decayed_keys.astype(jnp.float32), value_float)
        fading = jnp.exp(block_total)[None, :, None, None]
        running = running * fading + state[None]
        finished = finished * fading
        closing = (jnp.remainder(block_id + 1, periods) == 0)[:, None, None, None]
        finished = jnp.where(closing, running, finished)
        running = jnp.where(closing, jnp.zeros_like(running), running)
        square = lax.optimization_barrier(jnp.mean(mixed * mixed, axis=-1, keepdims=True))
        normed = mixed * lax.rsqrt(square + 1e-05) * gain_rows[:, None, :]
        output_rows = normed.transpose(1, 0, 2).reshape(SPAN, HEADS * HEAD).astype(jnp.bfloat16)
        return ((running, finished), output_rows)
    empty_state = jnp.zeros((upper_levels, HEADS, KEY, HEAD), jnp.float32)
    block_ids = jnp.arange(block_count, dtype=jnp.int32)
    final_carry, outputs = lax.scan(advance, (empty_state, empty_state), (query_blocks, key_blocks, value_blocks, decay_blocks, weight_blocks, block_ids))
    return outputs.reshape(TOKEN_COUNT, HEADS * HEAD)
```

```python
import functools

import jax
import jax.numpy as jnp
from jax import lax
from jax.experimental import pallas as pl
from jax.experimental.pallas import tpu as pltpu
from jax.sharding import PartitionSpec as P

MESH = pl.DeviceIdType.MESH
F32 = jnp.float32
BF16 = jnp.bfloat16
SPAN = 256
CHUNK = 128
VMEM = pl.BlockSpec(memory_space=pltpu.VMEM)


def lane(x, index):
    return jnp.broadcast_to(x[:, index : index + 1], x.shape)


def local_kernel(q_ref, k_ref, v_ref, d_ref, w_ref, acc_ref, ext_ref, cum_ref, qt_ref, span_s, half_s, u_s):
    heads, tokens = d_ref.shape
    chunks = tokens // CHUNK
    spans = tokens // SPAN
    rows = lax.broadcasted_iota(jnp.int32, (CHUNK, CHUNK), 0)
    cols = lax.broadcasted_iota(jnp.int32, (CHUNK, CHUNK), 1)
    causal = rows <= cols
    stacked = jnp.concatenate([d_ref[:, m * CHUNK : (m + 1) * CHUNK] for m in range(chunks)], axis=0)
    sums = jnp.dot(stacked, causal.astype(F32), precision=lax.Precision.HIGHEST, preferred_element_type=F32)
    inside = [sums[m * heads : (m + 1) * heads] for m in range(chunks)]
    totals = [lane(x, CHUNK - 1) for x in inside]
    before = jnp.zeros_like(totals[0])
    for m in range(chunks):
        cum_ref[:, m * CHUNK : (m + 1) * CHUNK] = before + inside[m]
        before = before + totals[m]
    span_total = [totals[2 * c] + totals[2 * c + 1] for c in range(spans)]
    qt_ref[...] = q_ref[...].astype(F32).T.astype(BF16)
    for m in range(chunks):
        at = slice(m * CHUNK, (m + 1) * CHUNK)
        c = m // 2
        if m % 2 == 1:
            u_s[0, :, at] = w_ref[0, :, at] * jnp.exp(inside[m])
        else:
            u_s[0, :, at] = jnp.zeros_like(inside[m])
        inner = inside[m] + totals[m - 1] if m % 2 == 1 else inside[m]
        u_s[1, :, at] = w_ref[1, :, at] * jnp.exp(inner)
        u_s[2, :, at] = w_ref[2, :, at] * jnp.exp(inner + span_total[2] if c == 3 else inner)
    for m in range(chunks):
        at = slice(m * CHUNK, (m + 1) * CHUNK)
        c = m // 2
        middle = lane(inside[m], CHUNK // 2 - 1)
        fade_out = jnp.exp(middle - inside[m]).astype(BF16)
        fade_in = w_ref[0, :, at] * jnp.exp(inside[m] - middle)
        rest = jnp.exp(totals[m] - middle)
        chunk_fade = jnp.exp(totals[m])
        keys = k_ref[at, :]
        scores = jnp.dot(keys, qt_ref[:, at], preferred_element_type=F32)
        right = jnp.concatenate([jnp.where(causal, scores, 0.0).astype(BF16), keys], axis=1)
        for h in range(heads):
            vt = v_ref[at, h * 128 : (h + 1) * 128].T
            out = jnp.dot(vt * fade_out[h : h + 1], right, preferred_element_type=F32)
            acc_ref[h, :, at] = out[:, :CHUNK] * fade_in[h : h + 1]
            state = out[:, CHUNK:] * rest[h : h + 1]
            if m % 2 == 0:
                half_s[c, h] = state
            else:
                span_s[c, h] = half_s[c, h] * chunk_fade[h : h + 1] + state
    fades = [jnp.exp(x) for x in span_total]
    all_total = before

    for h in range(heads):
        qt = qt_ref[...]

        def scaled(level, c):
            at = slice(c * SPAN, (c + 1) * SPAN)
            return qt[:, at] * u_s[level, h : h + 1, at].astype(BF16)

        first = span_s[0, h]
        pair = first * fades[1][h : h + 1] + span_s[1, h]
        triple = pair * fades[2][h : h + 1] + span_s[2, h]
        whole = triple * fades[3][h : h + 1] + span_s[3, h]
        ext_ref[h % 2, h // 2, :128] = whole
        ext_ref[h % 2, h // 2, 128:] = jnp.concatenate([all_total] * (8 // heads), axis=0)
        parts = [[], [(1, first)], [(2, pair)], [(1, span_s[2, h]), (2, pair)]]
        for c in range(spans):
            at = slice(c * SPAN, (c + 1) * SPAN)
            items = [(0, half_s[c, h])] + parts[c]
            left = jnp.concatenate([x.astype(BF16) for _, x in items], axis=1)
            right = jnp.concatenate([scaled(level, c) for level, _ in items], axis=0)
            acc_ref[h, :, at] += jnp.dot(left, right, preferred_element_type=F32)


def local_part(queries, keys, values, log_decay, level_weight):
    tokens = queries.shape[0]
    heads = log_decay.shape[0]
    return pl.pallas_call(
        local_kernel,
        out_shape=(
            jax.ShapeDtypeStruct((heads, 128, tokens), F32),
            jax.ShapeDtypeStruct((2, heads // 2, 136, 128), F32),
            jax.ShapeDtypeStruct((heads, tokens), F32),
            jax.ShapeDtypeStruct((128, tokens), BF16),
        ),
        in_specs=[VMEM] * 5,
        out_specs=(VMEM,) * 4,
        scratch_shapes=[
            pltpu.VMEM((tokens // SPAN, heads, 128, 128), F32),
            pltpu.VMEM((tokens // SPAN, heads, 128, 128), F32),
            pltpu.VMEM((3, heads, tokens), F32),
        ],
    )(queries, keys, values, log_decay, level_weight)


def bits_of(n):
    return n.bit_length() - 1


def tree(states, fades):
    found = []
    states, fades = list(states), list(fades)
    while len(states) > 1:
        found.append(states[0::2])
        states = [states[i] * fades[i + 1] + states[i + 1] for i in range(0, len(states), 2)]
        fades = [fades[i] * fades[i + 1] for i in range(0, len(fades), 2)]
    return found, states[0]


def pick(items, index):
    out = items[0]
    for i in range(1, len(items)):
        out = jnp.where(index == i, items[i], out)
    return out


def prefixes(totals, index):
    out = []
    running = jnp.zeros_like(totals[0])
    for bit in range(bits_of(len(totals))):
        out.append(running)
        low = lax.rem(index, 2 ** (bit + 1))
        upper = low >= 2**bit
        start = index - low
        side = jnp.zeros_like(running)
        for i in range(len(totals)):
            inside = jnp.logical_and(i >= start, i < start + 2**bit)
            side = side + jnp.where(inside, totals[i], 0.0)
        running = running + jnp.where(upper, side, 0.0)
    return out, running


def trade_kernel(
    ny, nx, nz, ext_ref, lev_ref, pre_ref,
    r1, gx, hz, lev, lvy, gbuf, hbuf, lvz,
    a_sem, p1_sem, p2_sem, p3_sem, y_sem, x_sem, z_sem, f_sem,
):
    nn = 2 * ny
    by, bx, bz = bits_of(ny), bits_of(nx), bits_of(nz)
    first_x = 1 + by
    first_z = first_x + bx
    part = 128 // nx
    n = lax.axis_index("narrow")
    wide = lax.axis_index("wide")
    y, c = n // 2, lax.rem(n, 2)
    z, x = wide // nx, lax.rem(wide, nx)
    mate = n + 1 - 2 * c

    def copy(src, dst, sems, index, to_n, to_wide):
        return pltpu.make_async_remote_copy(
            src_ref=src, dst_ref=dst, send_sem=sems.at[0, index], recv_sem=sems.at[1, index],
            device_id={"narrow": to_n, "wide": to_wide}, device_id_type=MESH,
        )

    barrier = pltpu.get_barrier_semaphore()
    peers = 0

    def hello(to_n, to_wide):
        pl.semaphore_signal(barrier, inc=1, device_id={"narrow": to_n, "wide": to_wide}, device_id_type=MESH)

    for o in range(1, nn):
        hello(lax.rem(n + o, nn), wide)
        peers += 1
    for o in range(1, nz):
        hello(n, lax.rem(z + o, nz) * nx + x)
        peers += 1
    for ox in range(1, nx):
        for oy in range(ny):
            hello(lax.rem(y + oy, ny) * 2 + c, z * nx + lax.rem(x + ox, nx))
            peers += 1
    pl.semaphore_wait(barrier, peers)

    level0 = copy(ext_ref.at[:, :, pl.ds(0, 128)], lev.at[0], a_sem, 0, mate, wide)

    @pl.when(c == 0)
    def _():
        level0.start()

    def p1(o):
        to = lax.rem(n + o, nn)
        return copy(ext_ref.at[lax.rem(to, 2), to // 2], r1.at[n], p1_sem, o, to, wide)

    for o in range(1, nn):
        p1(o).start()
    r1[n] = ext_ref[c, y]
    for o in range(1, nn):
        source = lax.rem(n + nn - o, nn)
        copy(r1.at[source], r1.at[source], p1_sem, o, n, wide).wait_recv()
    states = [r1[i, :128] for i in range(nn)]
    fades = [jnp.exp(r1[i, pl.ds(128 + n, 1)]) for i in range(nn)]
    narrow_totals = [r1[i, 128:] for i in range(nn)]
    found, group = tree(states, fades)
    gbuf[:128] = group
    group_total = narrow_totals[0]
    for i in range(1, nn):
        group_total = group_total + narrow_totals[i]
    gbuf[128:] = group_total

    def p2(o):
        return copy(gbuf, gx.at[x], p2_sem, o, n, z * nx + lax.rem(x + o, nx))

    for o in range(1, nx):
        p2(o).start()
    slot = 0
    slots = []
    for bit in range(by):
        slots.append(slot)
        for item in found[1 + bit]:
            lvy[slot] = item
            slot += 1

    def y_copy(bit, o):
        to = lax.rem(y + o, ny)
        return copy(
            lvy.at[slots[bit] + to // 2 ** (bit + 1)], lev.at[1 + bit, c, y], y_sem, bit * ny + o, to * 2 + c, wide
        )

    def has(index, bit):
        return lax.rem(index // 2**bit, 2) == 1

    for bit in range(by):
        for o in range(1, ny):

            @pl.when(has(lax.rem(y + o, ny), bit))
            def _():
                y_copy(bit, o).start()

        @pl.when(has(y, bit))
        def _():
            lev[1 + bit, c, y] = lvy[slots[bit] + y // 2 ** (bit + 1)]

        @pl.when(jnp.logical_not(has(y, bit)))
        def _():
            lev[1 + bit] = jnp.zeros(lev.shape[1:], F32)

    @pl.when(c == 0)
    def _():
        lev[0] = jnp.zeros(lev.shape[1:], F32)

    gx[x] = gbuf[...]
    for o in range(1, nx):
        source = lax.rem(x + nx - o, nx)
        copy(gx.at[source], gx.at[source], p2_sem, o, n, wide).wait_recv()
    states = [gx[i, :128] for i in range(nx)]
    fades = [jnp.exp(gx[i, pl.ds(128 + n, 1)]) for i in range(nx)]
    x_totals = [gx[i, 128:] for i in range(nx)]
    found, plane = tree(states, fades)
    hbuf_total = x_totals[0]
    for i in range(1, nx):
        hbuf_total = hbuf_total + x_totals[i]
    gbuf_rows = pl.ds(pl.multiple_of(x * part, part), part)
    r1[0, :128] = plane
    hbuf[:part] = r1[0, gbuf_rows]
    hbuf[part:] = hbuf_total

    def p3(o):
        return copy(hbuf, hz.at[z], p3_sem, o, n, lax.rem(z + o, nz) * nx + x)

    for o in range(1, nz):
        p3(o).start()
    for bit in range(bx):
        value = pick(found[bit], x // 2 ** (bit + 1))
        lev[first_x + bit, c, y] = jnp.where(has(x, bit), value, 0.0)

    def x_copy(o):
        block = lev.at[pl.ds(first_x, bx), c, y]
        return copy(block, block, x_sem, o, lax.rem(y + o, ny) * 2 + c, wide)

    for o in range(1, ny):
        x_copy(o).start()

    def forward(first, count, index):
        block = lev.at[pl.ds(first, count), c]
        return copy(block, block, f_sem, index, mate, wide)

    def forwarded(first, count, index):
        block = lev.at[pl.ds(first, count), 1 - c]
        return copy(block, block, f_sem, index, mate, wide)

    for bit in range(by):

        @pl.when(has(y, bit))
        def _():
            for o in range(1, ny):
                source = lax.rem(y + ny - o, ny)
                block = lev.at[1 + bit, c, source]
                copy(block, block, y_sem, bit * ny + o, n, wide).wait_recv()
            forward(1 + bit, 1, bit).start()

    hz[z] = hbuf[...]
    for o in range(1, nz):
        source = lax.rem(z + nz - o, nz)
        copy(hz.at[source], hz.at[source], p3_sem, o, n, wide).wait_recv()
    states = [hz[i, :part] for i in range(nz)]
    fades = [jnp.exp(hz[i, pl.ds(part + n, 1)]) for i in range(nz)]
    z_totals = [hz[i, part:] for i in range(nz)]
    found, _ = tree(states, fades)
    for bit in range(bz):
        value = pick(found[bit], z // 2 ** (bit + 1))
        lvz[bit] = jnp.where(has(z, bit), value, 0.0)

    def z_block(from_y, from_x):
        return lev.at[pl.ds(first_z, bz), c, from_y, pl.ds(pl.multiple_of(from_x * part, part), part)]

    def z_copy(ox, oy):
        return copy(
            lvz, z_block(y, x), z_sem, ox * ny + oy,
            lax.rem(y + oy, ny) * 2 + c, z * nx + lax.rem(x + ox, nx),
        )

    others = [(ox, oy) for ox in range(nx) for oy in range(ny) if ox or oy]
    for ox, oy in others:
        z_copy(ox, oy).start()
    for bit in range(bz):
        lev[first_z + bit, c, y, gbuf_rows] = lvz[bit]

    for o in range(1, ny):
        block = lev.at[pl.ds(first_x, bx), c, lax.rem(y + ny - o, ny)]
        copy(block, block, x_sem, o, n, wide).wait_recv()
    forward(first_x, bx, by).start()

    low, running = prefixes(narrow_totals, n)
    middle, x_running = prefixes(x_totals, x)
    high, _ = prefixes(z_totals, z)
    for i, item in enumerate(low):
        pre_ref[i] = item[:nn]
    for i, item in enumerate(middle):
        pre_ref[first_x + i] = (running + item)[:nn]
    for i, item in enumerate(high):
        pre_ref[first_z + i] = (running + x_running + item)[:nn]

    for bit in range(by):

        @pl.when(has(y, bit))
        def _():
            forwarded(1 + bit, 1, bit).wait_recv()

    @pl.when(c == 1)
    def _():
        level0.wait_recv()

    forwarded(first_x, bx, by).wait_recv()

    def put(level):
        for h in range(nn):
            lev_ref[h, :, level * 128 : (level + 1) * 128] = lev[level, h % 2, h // 2].astype(BF16)

    for level in range(first_z):
        put(level)
    for ox, oy in others:
        block = z_block(lax.rem(y + ny - oy, ny), lax.rem(x + nx - ox, nx))
        copy(block, block, z_sem, ox * ny + oy, n, wide).wait_recv()
    forward(first_z, bz, by + 1).start()
    forwarded(first_z, bz, by + 1).wait_recv()
    for level in range(first_z, first_z + bz):
        put(level)

    @pl.when(c == 0)
    def _():
        level0.wait_send()

    for o in range(1, nn):
        p1(o).wait_send()
    for o in range(1, nx):
        p2(o).wait_send()
    for o in range(1, nz):
        p3(o).wait_send()
    for o in range(1, ny):
        x_copy(o).wait_send()
    for ox, oy in others:
        z_copy(ox, oy).wait_send()
    for bit in range(by):
        for o in range(1, ny):

            @pl.when(has(lax.rem(y + o, ny), bit))
            def _():
                y_copy(bit, o).wait_send()

        @pl.when(has(y, bit))
        def _():
            forward(1 + bit, 1, bit).wait_send()

    forward(first_x, bx, by).wait_send()
    forward(first_z, bz, by + 1).wait_send()


def trade_part(ext, ny, nx, nz):
    heads = 2 * ny
    levels = 1 + bits_of(ny) + bits_of(nx) + bits_of(nz)
    part = 128 // nx
    dma = pltpu.SemaphoreType.DMA
    return pl.pallas_call(
        functools.partial(trade_kernel, ny, nx, nz),
        out_shape=(
            jax.ShapeDtypeStruct((heads, 128, levels * 128), BF16),
            jax.ShapeDtypeStruct((levels, heads, 128), F32),
        ),
        in_specs=[VMEM],
        out_specs=(VMEM, VMEM),
        scratch_shapes=[
            pltpu.VMEM((heads, 136, 128), F32),
            pltpu.VMEM((nx, 136, 128), F32),
            pltpu.VMEM((nz, part + 8, 128), F32),
            pltpu.VMEM((levels, 2, ny, 128, 128), F32),
            pltpu.VMEM((ny, 128, 128), F32),
            pltpu.VMEM((136, 128), F32),
            pltpu.VMEM((part + 8, 128), F32),
            pltpu.VMEM((bits_of(nz), part, 128), F32),
            dma((2, 1)),
            dma((2, heads)),
            dma((2, nx)),
            dma((2, nz)),
            dma((2, bits_of(ny) * ny)),
            dma((2, ny)),
            dma((2, nx * ny)),
            dma((2, bits_of(ny) + 2)),
        ],
        compiler_params=pltpu.CompilerParams(collective_id=0, has_side_effects=True),
    )(ext)


def finish_kernel(first, qt_ref, lev_ref, pre_ref, cum_ref, w_ref, acc_ref, gain_ref, out_ref):
    heads, tokens = cum_ref.shape
    levels = pre_ref.shape[0]
    gain = gain_ref[...]
    for h in range(heads):
        for c in range(tokens // SPAN):
            at = slice(c * SPAN, (c + 1) * SPAN)
            qt = qt_ref[:, at]
            cum = cum_ref[h : h + 1, at]
            right = []
            for level in range(levels):
                pre = pre_ref[level, h : h + 1, :]
                pre = jnp.concatenate([pre, pre], axis=1)
                scale = w_ref[first + level, h : h + 1, at] * jnp.exp(cum + pre)
                right.append(qt * scale.astype(BF16))
            mixed = acc_ref[h, :, at] + jnp.dot(
                lev_ref[h], jnp.concatenate(right, axis=0), preferred_element_type=F32
            )
            square = jnp.mean(mixed * mixed, axis=0, keepdims=True)
            normed = (mixed * lax.rsqrt(square + 1e-05)).T
            out_ref[at, h * 128 : (h + 1) * 128] = (normed * gain[:, h * 128 : (h + 1) * 128]).astype(BF16)


def finish_part(first, qt, lev, pre, cum, level_weight, acc, gain):
    heads, tokens = cum.shape
    return pl.pallas_call(
        functools.partial(finish_kernel, first),
        out_shape=jax.ShapeDtypeStruct((tokens, heads * 128), BF16),
        in_specs=[VMEM] * 7,
        out_specs=VMEM,
    )(qt, lev, pre, cum, level_weight, acc, gain)


def per_device(sizes, queries, keys, values, log_decay, level_weight, norm_gain):
    ny, nx, nz = sizes
    acc, ext, cum, qt = local_part(queries, keys, values, log_decay, level_weight)
    lev, pre = trade_part(ext, ny, nx, nz)
    first = level_weight.shape[0] - pre.shape[0]
    return finish_part(first, qt, lev, pre, cum, level_weight, acc, norm_gain.reshape(1, -1))


def solution(mesh, nx=4):
    sizes = (mesh.shape["narrow"] // 2, nx, mesh.shape["wide"] // nx)
    placed = (
        P(("wide", "narrow"), None),
        P(("wide", "narrow"), None),
        P(("wide", "narrow"), None),
        P(None, ("wide", "narrow")),
        P(None, None, ("wide", "narrow")),
        P(),
    )
    return jax.shard_map(
        functools.partial(per_device, sizes),
        mesh=mesh,
        in_specs=placed,
        out_specs=P(("wide", "narrow"), None),
        check_vma=False,
    )
```

```python
import functools

import jax
import jax.numpy as jnp
from jax import lax
from jax.experimental import pallas as pl
from jax.experimental.pallas import tpu as pltpu
from jax.sharding import PartitionSpec as P

MESH = pl.DeviceIdType.MESH
F32 = jnp.float32
BF16 = jnp.bfloat16
SPAN = 256
CHUNK = 128
VMEM = pl.BlockSpec(memory_space=pltpu.VMEM)


def lane(x, index):
    return jnp.broadcast_to(x[:, index : index + 1], x.shape)


def columns(index, width):
    return pl.ds(pl.multiple_of(index * width, width), width)


def bits_of(n):
    return n.bit_length() - 1


def tree(states, fades):
    found = []
    states, fades = list(states), list(fades)
    while len(states) > 1:
        found.append(states[0::2])
        states = [states[i] * fades[i + 1] + states[i + 1] for i in range(0, len(states), 2)]
        fades = [fades[i] * fades[i + 1] for i in range(0, len(fades), 2)]
    return found, states[0]


def pick(items, index):
    out = items[0]
    for i in range(1, len(items)):
        out = jnp.where(index == i, items[i], out)
    return out


def prefixes(totals, index):
    out = []
    running = jnp.zeros_like(totals[0])
    for bit in range(bits_of(len(totals))):
        out.append(running)
        low = lax.rem(index, 2 ** (bit + 1))
        upper = low >= 2**bit
        start = index - low
        side = jnp.zeros_like(running)
        for i in range(len(totals)):
            inside = jnp.logical_and(i >= start, i < start + 2**bit)
            side = side + jnp.where(inside, totals[i], 0.0)
        running = running + jnp.where(upper, side, 0.0)
    return out, running


def main_kernel(
    ny, nx, nz, q_hbm, k_hbm, v_hbm, d_hbm, w_hbm, acc_ref, lev_ref, pre_ref, cum_ref, qt_ref,
    ext, mate_buf, chip_buf, r1, gq, gxq, gbuf, gx, hbuf, hz, lev, lvy, lvz, rights, span_s, half_s, rows_s, u_s,
    e_sem, a_sem, p1_sem, p2_sem, g_sem, p3_sem, y_sem, x_sem, z_sem, f_sem, in_sem,
    q_ref, k_ref, v_ref, d_ref, w_ref,
):
    heads, tokens = d_ref.shape
    chunks, spans = tokens // CHUNK, tokens // SPAN
    local = bits_of(spans)
    by, bx, bz = bits_of(ny), bits_of(nx), bits_of(nz)
    first_x = 1 + by
    first_z = first_x + bx
    part = 128 // nx
    n = lax.axis_index("narrow")
    wide = lax.axis_index("wide")
    y, c = n // 2, lax.rem(n, 2)
    z, x = wide // nx, lax.rem(wide, nx)
    mate = n + 1 - 2 * c
    own_rows = pl.ds(pl.multiple_of(x * part, part), part)

    def copy(src, dst, sems, index, to_n, to_wide):
        return pltpu.make_async_remote_copy(
            src_ref=src, dst_ref=dst, send_sem=sems.at[0, index], recv_sem=sems.at[1, index],
            device_id={"narrow": to_n, "wide": to_wide}, device_id_type=MESH,
        )

    def has(index, bit):
        return lax.rem(index // 2**bit, 2) == 1

    fetches = [
        pltpu.make_async_copy(src, dst, in_sem.at[i])
        for i, (src, dst) in enumerate(
            [(d_hbm, d_ref), (k_hbm, k_ref), (v_hbm, v_ref), (q_hbm, q_ref), (w_hbm, w_ref)]
        )
    ]
    for fetch in fetches:
        fetch.start()

    barrier = pltpu.get_barrier_semaphore()
    peers = 0

    def hello(to_n, to_wide):
        pl.semaphore_signal(barrier, inc=1, device_id={"narrow": to_n, "wide": to_wide}, device_id_type=MESH)

    for o in range(1, nz):
        hello(n, lax.rem(z + o, nz) * nx + x)
        peers += 1
    for ox in range(nx):
        for oy in range(ny):
            if ox or oy:
                hello(lax.rem(y + oy, ny) * 2 + c, z * nx + lax.rem(x + ox, nx))
                peers += 1
    hello(mate, wide)
    peers += 1

    fetches[0].wait()
    at = [slice(m * CHUNK, (m + 1) * CHUNK) for m in range(chunks)]
    causal = lax.broadcasted_iota(jnp.int32, (CHUNK, CHUNK), 0) <= lax.broadcasted_iota(jnp.int32, (CHUNK, CHUNK), 1)
    stacked = jnp.concatenate([d_ref[:, at[m]] for m in range(chunks)], axis=0)
    sums = jnp.dot(stacked, causal.astype(F32), precision=lax.Precision.HIGHEST, preferred_element_type=F32)
    inside = [sums[m * heads : (m + 1) * heads] for m in range(chunks)]
    totals = [lane(v, CHUNK - 1) for v in inside]
    before = jnp.zeros_like(totals[0])
    for m in range(chunks):
        cum_ref[:, at[m]] = before + inside[m]
        before = before + totals[m]
    own_total = jnp.concatenate([before] * (8 // heads), axis=0)
    after = jnp.zeros_like(before)
    fades = [None] * chunks
    for m in reversed(range(chunks)):
        fades[m] = jnp.exp(after + (totals[m] - inside[m]))
        after = after + totals[m]

    fetches[1].wait()
    kt = k_ref[...].astype(F32).T
    fade = jnp.concatenate(fades, axis=1)
    fetches[2].wait()
    for h in range(heads):
        keys = (kt * fade[h : h + 1]).astype(BF16)
        state = jnp.dot(keys, v_ref[:, h * 128 : (h + 1) * 128], preferred_element_type=F32)
        ext[h % 2, h // 2, :128] = state.T
        ext[h % 2, h // 2, 128:] = own_total

    pl.semaphore_wait(barrier, peers)

    swap = copy(ext.at[1 - c], mate_buf, e_sem, 0, mate, wide)
    swap.start()
    level0 = copy(ext.at[:, :, pl.ds(0, 128)], lev.at[0], a_sem, 0, mate, wide)

    @pl.when(c == 0)
    def _():
        level0.start()

    @pl.when(c == 0)
    def _():
        lev[0] = jnp.zeros(lev.shape[1:], F32)

    swap.wait_recv()
    mate_total = mate_buf[0, 128:]
    for j in range(ny):
        mine = ext[c, j]
        theirs = mate_buf[j]
        row = pl.ds(128 + 2 * j + c, 1)
        left = jnp.where(c == 0, jnp.exp(mate_buf[j, row]), 1.0)
        right = jnp.where(c == 0, 1.0, jnp.exp(ext[c, j, row]))
        chip_buf[j, :128] = mine[:128] * left + theirs[:128] * right
        chip_buf[j, 128:] = mine[128:] + theirs[128:]

    def p1(o):
        to = lax.rem(y + o, ny)
        return copy(chip_buf.at[to], r1.at[y], p1_sem, o, to * 2 + c, wide)

    for o in range(1, ny):
        p1(o).start()

    fetches[3].wait()
    fetches[4].wait()
    qt_ref[...] = q_ref[...].astype(F32).T
    for m in range(chunks):
        keys = k_ref[at[m], :]
        scores = jnp.dot(keys, qt_ref[:, at[m]].astype(BF16), preferred_element_type=F32)
        rights[m] = jnp.concatenate([jnp.where(causal, scores, 0.0).astype(BF16), keys], axis=1)
        middle = lane(inside[m], CHUNK // 2 - 1)
        rows_s[0, :, at[m]] = jnp.exp(middle - inside[m])
        rows_s[1, :, at[m]] = w_ref[0, :, at[m]] * jnp.exp(inside[m] - middle)
        rows_s[2, :, at[m]] = jnp.exp(totals[m] - middle)
        rows_s[3, :, at[m]] = jnp.exp(totals[m])
    span_total = [totals[2 * i] + totals[2 * i + 1] for i in range(spans)]
    for m in range(chunks):
        inner = inside[m] + totals[m - 1] if m % 2 == 1 else inside[m]
        u_s[0, :, at[m]] = w_ref[0, :, at[m]] * jnp.exp(inside[m]) if m % 2 == 1 else jnp.zeros_like(inner)
        u_s[1, :, at[m]] = w_ref[1, :, at[m]] * jnp.exp(inner)
        u_s[2, :, at[m]] = w_ref[2, :, at[m]] * jnp.exp(inner + span_total[2] if m // 2 == 3 else inner)

    def chunk_products(h, carry):
        one = pl.ds(h, 1)
        out_row, in_row, rest_row, whole_row = [rows_s[i, one, :] for i in range(4)]
        for m in range(chunks):
            vt = v_ref[at[m], columns(h, 128)].T.astype(F32)
            left = (vt * out_row[:, at[m]]).astype(BF16)
            out = jnp.dot(left, rights[m], preferred_element_type=F32)
            acc_ref[h, :, at[m]] = out[:, :CHUNK] * in_row[:, at[m]]
            state = out[:, CHUNK:] * rest_row[:, at[m]]
            if m % 2 == 0:
                half_s[m // 2, h] = state
            else:
                span_s[m // 2, h] = half_s[m // 2, h] * whole_row[:, at[m]] + state
        return carry

    lax.fori_loop(0, heads, chunk_products, 0)

    r1[y] = chip_buf[y]
    for o in range(1, ny):
        source = lax.rem(y + ny - o, ny)
        copy(r1.at[source], r1.at[source], p1_sem, o, n, wide).wait_recv()
    chip_totals = [r1[i, 128:] for i in range(ny)]
    found, group = tree([r1[i, :128] for i in range(ny)], [jnp.exp(r1[i, pl.ds(128 + n, 1)]) for i in range(ny)])
    group_total = chip_totals[0]
    for i in range(1, ny):
        group_total = group_total + chip_totals[i]
    for i in range(nx):
        gq[i, :part] = group[i * part : (i + 1) * part]
        gq[i, part:] = group_total
    gbuf[...] = group

    def p2(o):
        to = lax.rem(x + o, nx)
        return copy(gq.at[to], gxq.at[x], p2_sem, o, n, z * nx + to)

    def whole_x(o):
        return copy(gbuf, gx.at[x], g_sem, o, n, z * nx + lax.rem(x + o, nx))

    for o in range(1, nx):
        p2(o).start()
    for o in range(1, nx):
        whole_x(o).start()
    slot = 0
    slots = []
    for bit in range(by):
        slots.append(slot)
        for item in found[bit]:
            lvy[slot] = item
            slot += 1

    def y_copy(bit, o):
        to = lax.rem(y + o, ny)
        return copy(
            lvy.at[slots[bit] + to // 2 ** (bit + 1)], lev.at[1 + bit, c, y], y_sem, bit * ny + o, to * 2 + c, wide
        )

    for bit in range(by):
        for o in range(1, ny):

            @pl.when(has(lax.rem(y + o, ny), bit))
            def _():
                y_copy(bit, o).start()

        @pl.when(has(y, bit))
        def _():
            lev[1 + bit, c, y] = lvy[slots[bit] + y // 2 ** (bit + 1)]

        @pl.when(jnp.logical_not(has(y, bit)))
        def _():
            lev[1 + bit] = jnp.zeros(lev.shape[1:], F32)

    gxq[x] = gq[x]
    gx[x] = gbuf[...]
    for o in range(1, nx):
        source = lax.rem(x + nx - o, nx)
        copy(gxq.at[source], gxq.at[source], p2_sem, o, n, wide).wait_recv()
    x_totals = [gxq[i, part:] for i in range(nx)]
    x_fades = [jnp.exp(gxq[i, pl.ds(part + n, 1)]) for i in range(nx)]
    _, plane = tree([gxq[i, :part] for i in range(nx)], x_fades)
    plane_total = x_totals[0]
    for i in range(1, nx):
        plane_total = plane_total + x_totals[i]
    hbuf[:part] = plane
    hbuf[part:] = plane_total

    def p3(o):
        return copy(hbuf, hz.at[z], p3_sem, o, n, lax.rem(z + o, nz) * nx + x)

    for o in range(1, nz):
        p3(o).start()

    for o in range(1, nx):
        source = lax.rem(x + nx - o, nx)
        copy(gx.at[source], gx.at[source], g_sem, o, n, wide).wait_recv()
    found, _ = tree([gx[i] for i in range(nx)], x_fades)
    for bit in range(bx):
        value = pick(found[bit], x // 2 ** (bit + 1))
        lev[first_x + bit, c, y] = jnp.where(has(x, bit), value, 0.0)

    def x_copy(o):
        block = lev.at[pl.ds(first_x, bx), c, y]
        return copy(block, block, x_sem, o, lax.rem(y + o, ny) * 2 + c, wide)

    for o in range(1, ny):
        x_copy(o).start()

    def forward(first, count, index):
        block = lev.at[pl.ds(first, count), c]
        return copy(block, block, f_sem, index, mate, wide)

    def forwarded(first, count, index):
        block = lev.at[pl.ds(first, count), 1 - c]
        return copy(block, block, f_sem, index, mate, wide)

    for bit in range(by):

        @pl.when(has(y, bit))
        def _():
            for o in range(1, ny):
                source = lax.rem(y + ny - o, ny)
                block = lev.at[1 + bit, c, source]
                copy(block, block, y_sem, bit * ny + o, n, wide).wait_recv()
            forward(1 + bit, 1, bit).start()

    hz[z] = hbuf[...]
    for o in range(1, nz):
        source = lax.rem(z + nz - o, nz)
        copy(hz.at[source], hz.at[source], p3_sem, o, n, wide).wait_recv()
    z_totals = [hz[i, part:] for i in range(nz)]
    found, _ = tree([hz[i, :part] for i in range(nz)], [jnp.exp(hz[i, pl.ds(part + n, 1)]) for i in range(nz)])
    for bit in range(bz):
        value = pick(found[bit], z // 2 ** (bit + 1))
        lvz[bit] = jnp.where(has(z, bit), value, 0.0)

    def z_block(from_y, from_x):
        return lev.at[pl.ds(first_z, bz), c, from_y, pl.ds(pl.multiple_of(from_x * part, part), part)]

    def z_copy(ox, oy):
        return copy(
            lvz, z_block(y, x), z_sem, ox * ny + oy,
            lax.rem(y + oy, ny) * 2 + c, z * nx + lax.rem(x + ox, nx),
        )

    others = [(ox, oy) for ox in range(nx) for oy in range(ny) if ox or oy]
    for ox, oy in others:
        z_copy(ox, oy).start()
    for bit in range(bz):
        lev[first_z + bit, c, y, own_rows] = lvz[bit]

    def local_levels(h, carry):
        one = pl.ds(h, 1)
        whole_row = rows_s[3, one, :]
        scales = [u_s[level, one, :] for level in range(3)]
        first = span_s[0, h]
        pair = first * (whole_row[:, at[2]] * whole_row[:, at[3]]) + span_s[1, h]
        parts = [[], [(1, first)], [(2, pair)], [(1, span_s[2, h]), (2, pair)]]
        for i in range(spans):
            here = slice(i * SPAN, (i + 1) * SPAN)
            items = [(0, half_s[i, h])] + parts[i]
            left = jnp.concatenate([v.astype(BF16) for _, v in items], axis=1)
            right = jnp.concatenate(
                [(qt_ref[:, here] * scales[level][:, here]).astype(BF16) for level, _ in items], axis=0
            )
            acc_ref[h, :, here] += jnp.dot(left, right, preferred_element_type=F32)
        return carry

    lax.fori_loop(0, heads, local_levels, 0)

    for o in range(1, ny):
        block = lev.at[pl.ds(first_x, bx), c, lax.rem(y + ny - o, ny)]
        copy(block, block, x_sem, o, n, wide).wait_recv()
    forward(first_x, bx, by).start()

    low = jnp.where(c == 1, mate_total, 0.0)
    chip_pre, y_running = prefixes(chip_totals, y)
    middle, x_running = prefixes(x_totals, x)
    high, _ = prefixes(z_totals, z)
    base = low + y_running
    pres = [jnp.zeros_like(low)] + [low + v for v in chip_pre]
    pres += [base + v for v in middle] + [base + x_running + v for v in high]
    for level, pre in enumerate(pres):
        pre_ref[level] = pre[:heads]
    for level in range(first_z):
        wide_pre = jnp.concatenate([pres[level][:heads]] * chunks, axis=1)
        u_s[1 + local + level] = w_ref[1 + local + level] * jnp.exp(cum_ref[...] + wide_pre)

    for bit in range(by):

        @pl.when(has(y, bit))
        def _():
            forwarded(1 + bit, 1, bit).wait_recv()

    @pl.when(c == 1)
    def _():
        level0.wait_recv()

    forwarded(first_x, bx, by).wait_recv()

    def outer_levels(h, carry):
        one = pl.ds(h, 1)
        left = jnp.concatenate(
            [lev[level, lax.rem(h, 2), h // 2].astype(BF16) for level in range(first_z)], axis=1
        )
        scales = [u_s[1 + local + level, one, :] for level in range(first_z)]
        for i in range(spans):
            here = slice(i * SPAN, (i + 1) * SPAN)
            right = jnp.concatenate(
                [(qt_ref[:, here] * scales[level][:, here]).astype(BF16) for level in range(first_z)], axis=0
            )
            acc_ref[h, :, here] += jnp.dot(left, right, preferred_element_type=F32)
        return carry

    lax.fori_loop(0, heads, outer_levels, 0)

    for ox, oy in others:
        block = z_block(lax.rem(y + ny - oy, ny), lax.rem(x + nx - ox, nx))
        copy(block, block, z_sem, ox * ny + oy, n, wide).wait_recv()
    forward(first_z, bz, by + 1).start()

    swap.wait_send()

    @pl.when(c == 0)
    def _():
        level0.wait_send()

    for o in range(1, ny):
        p1(o).wait_send()
        x_copy(o).wait_send()
    for o in range(1, nx):
        p2(o).wait_send()
        whole_x(o).wait_send()
    for o in range(1, nz):
        p3(o).wait_send()
    for ox, oy in others:
        z_copy(ox, oy).wait_send()
    for bit in range(by):
        for o in range(1, ny):

            @pl.when(has(lax.rem(y + o, ny), bit))
            def _():
                y_copy(bit, o).wait_send()

        @pl.when(has(y, bit))
        def _():
            forward(1 + bit, 1, bit).wait_send()

    forward(first_x, bx, by).wait_send()
    forwarded(first_z, bz, by + 1).wait_recv()
    for level in range(bz):
        for h in range(heads):
            lev_ref[h, :, level * 128 : (level + 1) * 128] = lev[first_z + level, h % 2, h // 2].astype(BF16)
    forward(first_z, bz, by + 1).wait_send()


def main_part(ny, nx, nz, queries, keys, values, log_decay, level_weight):
    heads, tokens = log_decay.shape
    by, bx, bz = bits_of(ny), bits_of(nx), bits_of(nz)
    levels = 1 + by + bx + bz
    chunks, spans = tokens // CHUNK, tokens // SPAN
    part = 128 // nx
    dma = pltpu.SemaphoreType.DMA
    return pl.pallas_call(
        functools.partial(main_kernel, ny, nx, nz),
        out_shape=(
            jax.ShapeDtypeStruct((heads, 128, tokens), F32),
            jax.ShapeDtypeStruct((heads, 128, bz * 128), BF16),
            jax.ShapeDtypeStruct((levels, heads, 128), F32),
            jax.ShapeDtypeStruct((heads, tokens), F32),
            jax.ShapeDtypeStruct((128, tokens), F32),
        ),
        in_specs=[pl.BlockSpec(memory_space=pltpu.HBM)] * 5,
        out_specs=(VMEM,) * 5,
        scratch_shapes=[
            pltpu.VMEM((2, ny, 136, 128), F32),
            pltpu.VMEM((ny, 136, 128), F32),
            pltpu.VMEM((ny, 136, 128), F32),
            pltpu.VMEM((ny, 136, 128), F32),
            pltpu.VMEM((nx, part + 8, 128), F32),
            pltpu.VMEM((nx, part + 8, 128), F32),
            pltpu.VMEM((128, 128), F32),
            pltpu.VMEM((nx, 128, 128), F32),
            pltpu.VMEM((part + 8, 128), F32),
            pltpu.VMEM((nz, part + 8, 128), F32),
            pltpu.VMEM((levels, 2, ny, 128, 128), F32),
            pltpu.VMEM((ny, 128, 128), F32),
            pltpu.VMEM((bz, part, 128), F32),
            pltpu.VMEM((chunks, CHUNK, 2 * CHUNK), BF16),
            pltpu.VMEM((spans, heads, 128, 128), F32),
            pltpu.VMEM((spans, heads, 128, 128), F32),
            pltpu.VMEM((4, heads, tokens), F32),
            pltpu.VMEM((1 + bits_of(spans) + 1 + by + bx, heads, tokens), F32),
            dma((2, 1)),
            dma((2, 1)),
            dma((2, ny)),
            dma((2, nx)),
            dma((2, nx)),
            dma((2, nz)),
            dma((2, by * ny)),
            dma((2, ny)),
            dma((2, nx * ny)),
            dma((2, by + 2)),
            dma((5,)),
            pltpu.VMEM(queries.shape, queries.dtype),
            pltpu.VMEM(keys.shape, keys.dtype),
            pltpu.VMEM(values.shape, values.dtype),
            pltpu.VMEM(log_decay.shape, log_decay.dtype),
            pltpu.VMEM(level_weight.shape, level_weight.dtype),
        ],
        compiler_params=pltpu.CompilerParams(collective_id=0, has_side_effects=True, vmem_limit_bytes=40 * 2**20),
    )(*[pltpu.with_memory_space_constraint(v, pltpu.HBM) for v in (queries, keys, values, log_decay, level_weight)])


def finish_kernel(skip, qt_ref, lev_ref, pre_ref, cum_ref, w_ref, acc_ref, gain_ref, out_ref):
    heads, tokens = cum_ref.shape
    levels = lev_ref.shape[2] // 128
    first = w_ref.shape[0] - levels
    gain = gain_ref[...]
    for h in range(heads):
        for i in range(tokens // SPAN):
            at = slice(i * SPAN, (i + 1) * SPAN)
            qt = qt_ref[:, at]
            cum = cum_ref[h : h + 1, at]
            right = []
            for level in range(levels):
                pre = pre_ref[skip + level, h : h + 1, :]
                pre = jnp.concatenate([pre, pre], axis=1)
                right.append((qt * (w_ref[first + level, h : h + 1, at] * jnp.exp(cum + pre))).astype(BF16))
            mixed = acc_ref[h, :, at] + jnp.dot(
                lev_ref[h], jnp.concatenate(right, axis=0), preferred_element_type=F32
            )
            square = jnp.mean(mixed * mixed, axis=0, keepdims=True)
            normed = (mixed * lax.rsqrt(square + 1e-05)).T
            out_ref[at, h * 128 : (h + 1) * 128] = (normed * gain[:, h * 128 : (h + 1) * 128]).astype(BF16)


def finish_part(skip, qt, lev, pre, cum, level_weight, acc, gain):
    heads, tokens = cum.shape
    return pl.pallas_call(
        functools.partial(finish_kernel, skip),
        out_shape=jax.ShapeDtypeStruct((tokens, heads * 128), BF16),
        in_specs=[VMEM] * 7,
        out_specs=VMEM,
        compiler_params=pltpu.CompilerParams(vmem_limit_bytes=24 * 2**20),
    )(qt, lev, pre, cum, level_weight, acc, gain)


def per_device(sizes, queries, keys, values, log_decay, level_weight, norm_gain):
    ny, nx, nz = sizes
    acc, lev, pre, cum, qt = main_part(ny, nx, nz, queries, keys, values, log_decay, level_weight)
    skip = pre.shape[0] - lev.shape[2] // 128
    return finish_part(skip, qt, lev, pre, cum, level_weight, acc, norm_gain.reshape(1, -1))


def solution(mesh, nx=4):
    sizes = (mesh.shape["narrow"] // 2, nx, mesh.shape["wide"] // nx)
    placed = (
        P(("wide", "narrow"), None),
        P(("wide", "narrow"), None),
        P(("wide", "narrow"), None),
        P(None, ("wide", "narrow")),
        P(None, None, ("wide", "narrow")),
        P(),
    )
    return jax.shard_map(
        functools.partial(per_device, sizes),
        mesh=mesh,
        in_specs=placed,
        out_specs=P(("wide", "narrow"), None),
        check_vma=False,
    )
```

```python
import functools

import jax
import jax.numpy as jnp
from jax import lax
from jax.experimental import pallas as pl
from jax.experimental.pallas import tpu as pltpu
from jax.sharding import PartitionSpec as P

MESH = pl.DeviceIdType.MESH
F32 = jnp.float32
BF16 = jnp.bfloat16
SPAN = 256
CHUNK = 128
VMEM = pl.BlockSpec(memory_space=pltpu.VMEM)


def lane(x, index):
    return jnp.broadcast_to(x[:, index : index + 1], x.shape)


def columns(index, width):
    return pl.ds(pl.multiple_of(index * width, width), width)


def bits_of(n):
    return n.bit_length() - 1


def tree(states, fades):
    found = []
    states, fades = list(states), list(fades)
    while len(states) > 1:
        found.append(states[0::2])
        states = [states[i] * fades[i + 1] + states[i + 1] for i in range(0, len(states), 2)]
        fades = [fades[i] * fades[i + 1] for i in range(0, len(fades), 2)]
    return found, states[0]


def pick(items, index):
    out = items[0]
    for i in range(1, len(items)):
        out = jnp.where(index == i, items[i], out)
    return out


def prefixes(totals, index):
    out = []
    running = jnp.zeros_like(totals[0])
    for bit in range(bits_of(len(totals))):
        out.append(running)
        low = lax.rem(index, 2 ** (bit + 1))
        upper = low >= 2**bit
        start = index - low
        side = jnp.zeros_like(running)
        for i in range(len(totals)):
            inside = jnp.logical_and(i >= start, i < start + 2**bit)
            side = side + jnp.where(inside, totals[i], 0.0)
        running = running + jnp.where(upper, side, 0.0)
    return out, running


def main_kernel(
    ny, nx, nz, q_hbm, k_hbm, v_hbm, d_hbm, w_hbm, gain_hbm, acc_ref, lev_ref, right_ref, gain_ref,
    ext, mate_buf, chip_buf, r1, gq, gxq, gbuf, gx, hbuf, hz, lev, lvy, lvz, rights, span_s, half_s, rows_s, u_s, cum_ref, qt_ref, fade_s,
    e_sem, a_sem, p1_sem, p2_sem, g_sem, p3_sem, y_sem, x_sem, z_sem, f_sem, in_sem,
    q_ref, k_ref, v_ref, d_ref, w_ref,
):
    heads, tokens = d_ref.shape
    chunks, spans = tokens // CHUNK, tokens // SPAN
    local = bits_of(spans)
    by, bx, bz = bits_of(ny), bits_of(nx), bits_of(nz)
    first_x = 1 + by
    first_z = first_x + bx
    part = 128 // nx
    n = lax.axis_index("narrow")
    wide = lax.axis_index("wide")
    y, c = n // 2, lax.rem(n, 2)
    z, x = wide // nx, lax.rem(wide, nx)
    mate = n + 1 - 2 * c
    own_rows = pl.ds(pl.multiple_of(x * part, part), part)

    def copy(src, dst, sems, index, to_n, to_wide):
        return pltpu.make_async_remote_copy(
            src_ref=src, dst_ref=dst, send_sem=sems.at[0, index], recv_sem=sems.at[1, index],
            device_id={"narrow": to_n, "wide": to_wide}, device_id_type=MESH,
        )

    def has(index, bit):
        return lax.rem(index // 2**bit, 2) == 1

    fetches = [
        pltpu.make_async_copy(src, dst, in_sem.at[i])
        for i, (src, dst) in enumerate(
            [
                (d_hbm, d_ref), (k_hbm, k_ref), (v_hbm, v_ref), (q_hbm, q_ref), (w_hbm, w_ref),
                (gain_hbm, gain_ref),
            ]
        )
    ]
    for fetch in fetches:
        fetch.start()

    barrier = pltpu.get_barrier_semaphore()
    peers = 0

    def hello(to_n, to_wide):
        pl.semaphore_signal(barrier, inc=1, device_id={"narrow": to_n, "wide": to_wide}, device_id_type=MESH)

    for o in range(1, nz):

        @pl.when(z >= o)
        def _():
            hello(n, (z - o) * nx + x)

    for ox in range(nx):
        for oy in range(ny):
            if ox or oy:
                hello(lax.rem(y + oy, ny) * 2 + c, z * nx + lax.rem(x + ox, nx))
                peers += 1
    hello(mate, wide)
    peers += 1

    fetches[0].wait()
    at = [slice(m * CHUNK, (m + 1) * CHUNK) for m in range(chunks)]
    causal = lax.broadcasted_iota(jnp.int32, (CHUNK, CHUNK), 0) <= lax.broadcasted_iota(jnp.int32, (CHUNK, CHUNK), 1)
    stacked = jnp.concatenate([d_ref[:, at[m]] for m in range(chunks)], axis=0)
    sums = jnp.dot(stacked, causal.astype(F32), precision=lax.Precision.HIGHEST, preferred_element_type=F32)
    inside = [sums[m * heads : (m + 1) * heads] for m in range(chunks)]
    totals = [lane(v, CHUNK - 1) for v in inside]
    before = jnp.zeros_like(totals[0])
    for m in range(chunks):
        cum_ref[:, at[m]] = before + inside[m]
        before = before + totals[m]
    own_total = jnp.concatenate([before] * (8 // heads), axis=0)
    after = jnp.zeros_like(before)
    fades = [None] * chunks
    for m in reversed(range(chunks)):
        fades[m] = jnp.exp(after + (totals[m] - inside[m]))
        after = after + totals[m]

    fetches[1].wait()
    kt = k_ref[...].astype(F32).T
    for m in range(chunks):
        fade_s[:, at[m]] = fades[m]
    fetches[2].wait()

    def states(odd):
        for j in range(ny):
            h = 2 * j + odd
            keys = (kt * fade_s[pl.ds(h, 1), :]).astype(BF16)
            state = jnp.dot(keys, v_ref[:, columns(h, 128)], preferred_element_type=F32)
            ext[odd, j, :128] = state.T
            ext[odd, j, 128:] = own_total

    states(1 - c)
    pl.semaphore_wait(barrier, peers + nz - 1 - z)
    swap = copy(ext.at[1 - c], mate_buf, e_sem, 0, mate, wide)
    swap.start()
    states(c)
    level0 = copy(ext.at[:, :, pl.ds(0, 128)], lev.at[0], a_sem, 0, mate, wide)

    @pl.when(c == 0)
    def _():
        level0.start()

    @pl.when(c == 0)
    def _():
        lev[0] = jnp.zeros(lev.shape[1:], F32)

    swap.wait_recv()
    mate_total = mate_buf[0, 128:]
    for j in range(ny):
        mine = ext[c, j]
        theirs = mate_buf[j]
        row = pl.ds(128 + 2 * j + c, 1)
        left = jnp.where(c == 0, jnp.exp(mate_buf[j, row]), 1.0)
        right = jnp.where(c == 0, 1.0, jnp.exp(ext[c, j, row]))
        chip_buf[j, :128] = mine[:128] * left + theirs[:128] * right
        chip_buf[j, 128:] = mine[128:] + theirs[128:]

    def p1(o):
        to = lax.rem(y + o, ny)
        return copy(chip_buf.at[to], r1.at[y], p1_sem, o, to * 2 + c, wide)

    for o in range(1, ny):
        p1(o).start()

    fetches[3].wait()
    fetches[4].wait()
    fetches[5].wait()
    qt_ref[...] = q_ref[...].astype(F32).T
    for m in range(chunks):
        keys = k_ref[at[m], :]
        scores = jnp.dot(keys, qt_ref[:, at[m]].astype(BF16), preferred_element_type=F32)
        rights[m] = jnp.concatenate([jnp.where(causal, scores, 0.0).astype(BF16), keys], axis=1)
        middle = lane(inside[m], CHUNK // 2 - 1)
        rows_s[0, :, at[m]] = jnp.exp(middle - inside[m])
        rows_s[1, :, at[m]] = w_ref[0, :, at[m]] * jnp.exp(inside[m] - middle)
        rows_s[2, :, at[m]] = jnp.exp(totals[m] - middle)
        rows_s[3, :, at[m]] = jnp.exp(totals[m])
    span_total = [totals[2 * i] + totals[2 * i + 1] for i in range(spans)]
    for m in range(chunks):
        inner = inside[m] + totals[m - 1] if m % 2 == 1 else inside[m]
        u_s[0, :, at[m]] = w_ref[0, :, at[m]] * jnp.exp(inside[m]) if m % 2 == 1 else jnp.zeros_like(inner)
        u_s[1, :, at[m]] = w_ref[1, :, at[m]] * jnp.exp(inner)
        u_s[2, :, at[m]] = w_ref[2, :, at[m]] * jnp.exp(inner + span_total[2] if m // 2 == 3 else inner)

    def chunk_products(h, carry):
        one = pl.ds(h, 1)
        out_row, in_row, rest_row, whole_row = [rows_s[i, one, :] for i in range(4)]
        for m in range(chunks):
            vt = v_ref[at[m], columns(h, 128)].T.astype(F32)
            left = (vt * out_row[:, at[m]]).astype(BF16)
            out = jnp.dot(left, rights[m], preferred_element_type=F32)
            acc_ref[h, :, at[m]] = out[:, :CHUNK] * in_row[:, at[m]]
            state = out[:, CHUNK:] * rest_row[:, at[m]]
            if m % 2 == 0:
                half_s[m // 2, h] = state
            else:
                span_s[m // 2, h] = half_s[m // 2, h] * whole_row[:, at[m]] + state
        return carry

    lax.fori_loop(0, heads, chunk_products, 0)

    r1[y] = chip_buf[y]
    for o in range(1, ny):
        source = lax.rem(y + ny - o, ny)
        copy(r1.at[source], r1.at[source], p1_sem, o, n, wide).wait_recv()
    chip_totals = [r1[i, 128:] for i in range(ny)]
    found, group = tree([r1[i, :128] for i in range(ny)], [jnp.exp(r1[i, pl.ds(128 + n, 1)]) for i in range(ny)])
    group_total = chip_totals[0]
    for i in range(1, ny):
        group_total = group_total + chip_totals[i]
    for i in range(nx):
        gq[i, :part] = group[i * part : (i + 1) * part]
        gq[i, part:] = group_total
    gbuf[...] = group

    def p2(o):
        to = lax.rem(x + o, nx)
        return copy(gq.at[to], gxq.at[x], p2_sem, o, n, z * nx + to)

    def whole_x(o):
        return copy(gbuf, gx.at[x], g_sem, o, n, z * nx + lax.rem(x + o, nx))

    for o in range(1, nx):
        p2(o).start()
    for o in range(1, nx):
        whole_x(o).start()
    slot = 0
    slots = []
    for bit in range(by):
        slots.append(slot)
        for item in found[bit]:
            lvy[slot] = item
            slot += 1

    def y_copy(bit, o):
        to = lax.rem(y + o, ny)
        return copy(
            lvy.at[slots[bit] + to // 2 ** (bit + 1)], lev.at[1 + bit, c, y], y_sem, bit * ny + o, to * 2 + c, wide
        )

    for bit in range(by):
        for o in range(1, ny):

            @pl.when(has(lax.rem(y + o, ny), bit))
            def _():
                y_copy(bit, o).start()

        @pl.when(has(y, bit))
        def _():
            lev[1 + bit, c, y] = lvy[slots[bit] + y // 2 ** (bit + 1)]

        @pl.when(jnp.logical_not(has(y, bit)))
        def _():
            lev[1 + bit] = jnp.zeros(lev.shape[1:], F32)

    gxq[x] = gq[x]
    gx[x] = gbuf[...]
    for o in range(1, nx):
        source = lax.rem(x + nx - o, nx)
        copy(gxq.at[source], gxq.at[source], p2_sem, o, n, wide).wait_recv()
    x_totals = [gxq[i, part:] for i in range(nx)]
    x_fades = [jnp.exp(gxq[i, pl.ds(part + n, 1)]) for i in range(nx)]
    _, plane = tree([gxq[i, :part] for i in range(nx)], x_fades)
    plane_total = x_totals[0]
    for i in range(1, nx):
        plane_total = plane_total + x_totals[i]
    hbuf[:part] = plane
    hbuf[part:] = plane_total

    def p3(o):
        return copy(hbuf, hz.at[z], p3_sem, o, n, (z + o) * nx + x)

    for o in range(1, nz):

        @pl.when(z + o < nz)
        def _():
            p3(o).start()

    for o in range(1, nx):
        source = lax.rem(x + nx - o, nx)
        copy(gx.at[source], gx.at[source], g_sem, o, n, wide).wait_recv()
    found, _ = tree([gx[i] for i in range(nx)], x_fades)

    def x_copy(bit, o):
        block = lev.at[first_x + bit, c, y]
        return copy(block, block, x_sem, bit * ny + o, lax.rem(y + o, ny) * 2 + c, wide)

    for bit in range(bx):

        @pl.when(has(x, bit))
        def _():
            lev[first_x + bit, c, y] = pick(found[bit], x // 2 ** (bit + 1))
            for o in range(1, ny):
                x_copy(bit, o).start()

        @pl.when(jnp.logical_not(has(x, bit)))
        def _():
            lev[first_x + bit] = jnp.zeros(lev.shape[1:], F32)

    def forward(first, count, index):
        block = lev.at[pl.ds(first, count), c]
        return copy(block, block, f_sem, index, mate, wide)

    def forwarded(first, count, index):
        block = lev.at[pl.ds(first, count), 1 - c]
        return copy(block, block, f_sem, index, mate, wide)

    for bit in range(by):

        @pl.when(has(y, bit))
        def _():
            for o in range(1, ny):
                source = lax.rem(y + ny - o, ny)
                block = lev.at[1 + bit, c, source]
                copy(block, block, y_sem, bit * ny + o, n, wide).wait_recv()
            forward(1 + bit, 1, bit).start()

    def z_block(count, from_y, from_x):
        rows = pl.ds(pl.multiple_of(from_x * part, part), part)
        return lev.at[pl.ds(first_z, count), c, from_y, rows]

    def z_copy(count, ox, oy):
        return copy(
            lvz.at[pl.ds(0, count)], z_block(count, y, x), z_sem, ox * ny + oy,
            lax.rem(y + oy, ny) * 2 + c, z * nx + lax.rem(x + ox, nx),
        )

    def z_forward(count, parity, ox):
        rows = pl.ds(pl.multiple_of(lax.rem(x + nx - ox, nx) * part, part), part)
        block = lev.at[pl.ds(first_z, count), parity, :, rows]
        return copy(block, block, f_sem, by + bx + ox, mate, wide)

    others = [(ox, oy) for ox in range(nx) for oy in range(ny) if ox or oy]
    near = sorted(range(nx), key=lambda o: min(o, nx - o))
    slot_of = [sum([lax.rem(z // 2**i, 2) for i in range(bit)], z * 0) for bit in range(bz)]
    held = sum([lax.rem(z // 2**i, 2) for i in range(bz)], z * 0)
    for o in range(1, nz):

        @pl.when(z >= o)
        def _():
            copy(hz.at[z - o], hz.at[z - o], p3_sem, o, n, wide).wait_recv()

    z_totals = [hz[i, part:] for i in range(nz)]
    found, _ = tree([hz[i, :part] for i in range(nz)], [jnp.exp(hz[i, pl.ds(part + n, 1)]) for i in range(nz)])
    for bit in range(bz):

        @pl.when(has(z, bit))
        def _():
            lvz[slot_of[bit]] = pick(found[bit], z // 2 ** (bit + 1))

    for count in range(1, bz + 1):

        @pl.when(held == count)
        def _():
            for ox, oy in others:
                z_copy(count, ox, oy).start()
            lev[first_z : first_z + count, c, y, own_rows] = lvz[:count]

    for slot in range(bz):

        @pl.when(held <= slot)
        def _():
            lev[first_z + slot] = jnp.zeros(lev.shape[1:], F32)

    def local_levels(h, carry):
        one = pl.ds(h, 1)
        whole_row = rows_s[3, one, :]
        scales = [u_s[level, one, :] for level in range(3)]
        first = span_s[0, h]
        pair = first * (whole_row[:, at[2]] * whole_row[:, at[3]]) + span_s[1, h]
        parts = [[], [(1, first)], [(2, pair)], [(1, span_s[2, h]), (2, pair)]]
        for i in range(spans):
            here = slice(i * SPAN, (i + 1) * SPAN)
            items = [(0, half_s[i, h])] + parts[i]
            left = jnp.concatenate([v.astype(BF16) for _, v in items], axis=1)
            right = jnp.concatenate(
                [(qt_ref[:, here] * scales[level][:, here]).astype(BF16) for level, _ in items], axis=0
            )
            acc_ref[h, :, here] += jnp.dot(left, right, preferred_element_type=F32)
        return carry

    low = jnp.where(c == 1, mate_total, 0.0)
    chip_pre, y_running = prefixes(chip_totals, y)
    middle, x_running = prefixes(x_totals, x)
    high, _ = prefixes(z_totals, z)
    base = low + y_running
    pres = [jnp.zeros_like(low)] + [low + v for v in chip_pre]
    pres += [base + v for v in middle] + [base + x_running + v for v in high]

    def scale(level):
        wide_pre = jnp.concatenate([pres[level][:heads]] * chunks, axis=1)
        return w_ref[1 + local + level] * jnp.exp(cum_ref[...] + wide_pre)

    for level in range(first_z):
        u_s[1 + local + level] = scale(level)
    for bit in range(bz):
        u_s[1 + local + first_z + bit] = jnp.zeros((heads, tokens), F32)
    for bit in range(bz):

        @pl.when(has(z, bit))
        def _():
            u_s[1 + local + first_z + slot_of[bit]] = scale(first_z + bit)

    def z_rights(h, carry):
        one = pl.ds(h, 1)
        for slot in range(bz):
            row = u_s[1 + local + first_z + slot, one, :]
            right_ref[h, slot * 128 : (slot + 1) * 128, :] = (qt_ref[...] * row).astype(BF16)
        return carry

    def level_products(levels):
        def body(h, carry):
            one = pl.ds(h, 1)
            left = jnp.concatenate([lev[level, lax.rem(h, 2), h // 2].astype(BF16) for level in levels], axis=1)
            scales = [u_s[1 + local + level, one, :] for level in levels]
            for i in range(spans):
                here = slice(i * SPAN, (i + 1) * SPAN)
                right = jnp.concatenate([(qt_ref[:, here] * row[:, here]).astype(BF16) for row in scales], axis=0)
                acc_ref[h, :, here] += jnp.dot(left, right, preferred_element_type=F32)
            return carry

        lax.fori_loop(0, heads, body, 0)

    lax.fori_loop(0, heads, z_rights, 0)
    lax.fori_loop(0, heads, local_levels, 0)
    for bit in range(by):

        @pl.when(has(y, bit))
        def _():
            forwarded(1 + bit, 1, bit).wait_recv()

    @pl.when(c == 1)
    def _():
        level0.wait_recv()

    level_products(range(first_x))

    for bit in range(bx):

        @pl.when(has(x, bit))
        def _():
            for o in range(1, ny):
                block = lev.at[first_x + bit, c, lax.rem(y + ny - o, ny)]
                copy(block, block, x_sem, bit * ny + o, n, wide).wait_recv()
            forward(first_x + bit, 1, by + bit).start()

    for count in range(1, bz + 1):

        @pl.when(held == count)
        def _():
            for ox in near:
                for oy in range(ny):
                    if ox or oy:
                        block = z_block(count, lax.rem(y + ny - oy, ny), lax.rem(x + nx - ox, nx))
                        copy(block, block, z_sem, ox * ny + oy, n, wide).wait_recv()
                z_forward(count, c, ox).start()

    for bit in range(bx):

        @pl.when(has(x, bit))
        def _():
            forwarded(first_x + bit, 1, by + bit).wait_recv()

    level_products(range(first_x, first_z))

    swap.wait_send()

    @pl.when(c == 0)
    def _():
        level0.wait_send()

    for o in range(1, ny):
        p1(o).wait_send()
    for o in range(1, nx):
        p2(o).wait_send()
        whole_x(o).wait_send()
    for o in range(1, nz):

        @pl.when(z + o < nz)
        def _():
            p3(o).wait_send()

    for bit in range(bx):

        @pl.when(has(x, bit))
        def _():
            for o in range(1, ny):
                x_copy(bit, o).wait_send()
            forward(first_x + bit, 1, by + bit).wait_send()

    for bit in range(by):
        for o in range(1, ny):

            @pl.when(has(lax.rem(y + o, ny), bit))
            def _():
                y_copy(bit, o).wait_send()

        @pl.when(has(y, bit))
        def _():
            forward(1 + bit, 1, bit).wait_send()

    for count in range(1, bz + 1):

        @pl.when(held == count)
        def _():
            for ox, oy in others:
                z_copy(count, ox, oy).wait_send()
            for ox in near:
                z_forward(count, 1 - c, ox).wait_recv()
            for ox in near:
                z_forward(count, c, ox).wait_send()

    for slot in range(bz):
        for h in range(heads):
            lev_ref[h, :, slot * 128 : (slot + 1) * 128] = lev[first_z + slot, h % 2, h // 2].astype(BF16)


def main_part(ny, nx, nz, queries, keys, values, log_decay, level_weight, gain):
    heads, tokens = log_decay.shape
    by, bx, bz = bits_of(ny), bits_of(nx), bits_of(nz)
    levels = 1 + by + bx + bz
    chunks, spans = tokens // CHUNK, tokens // SPAN
    part = 128 // nx
    dma = pltpu.SemaphoreType.DMA
    return pl.pallas_call(
        functools.partial(main_kernel, ny, nx, nz),
        out_shape=(
            jax.ShapeDtypeStruct((heads, 128, tokens), F32),
            jax.ShapeDtypeStruct((heads, 128, bz * 128), BF16),
            jax.ShapeDtypeStruct((heads, bz * 128, tokens), BF16),
            jax.ShapeDtypeStruct(gain.shape, F32),
        ),
        in_specs=[pl.BlockSpec(memory_space=pltpu.HBM)] * 6,
        out_specs=(VMEM,) * 4,
        scratch_shapes=[
            pltpu.VMEM((2, ny, 136, 128), F32),
            pltpu.VMEM((ny, 136, 128), F32),
            pltpu.VMEM((ny, 136, 128), F32),
            pltpu.VMEM((ny, 136, 128), F32),
            pltpu.VMEM((nx, part + 8, 128), F32),
            pltpu.VMEM((nx, part + 8, 128), F32),
            pltpu.VMEM((128, 128), F32),
            pltpu.VMEM((nx, 128, 128), F32),
            pltpu.VMEM((part + 8, 128), F32),
            pltpu.VMEM((nz, part + 8, 128), F32),
            pltpu.VMEM((levels, 2, ny, 128, 128), F32),
            pltpu.VMEM((ny, 128, 128), F32),
            pltpu.VMEM((bz, part, 128), F32),
            pltpu.VMEM((chunks, CHUNK, 2 * CHUNK), BF16),
            pltpu.VMEM((spans, heads, 128, 128), F32),
            pltpu.VMEM((spans, heads, 128, 128), F32),
            pltpu.VMEM((4, heads, tokens), F32),
            pltpu.VMEM((1 + bits_of(spans) + levels, heads, tokens), F32),
            pltpu.VMEM((heads, tokens), F32),
            pltpu.VMEM((128, tokens), F32),
            pltpu.VMEM((heads, tokens), F32),
            dma((2, 1)),
            dma((2, 1)),
            dma((2, ny)),
            dma((2, nx)),
            dma((2, nx)),
            dma((2, nz)),
            dma((2, by * ny)),
            dma((2, bx * ny)),
            dma((2, nx * ny)),
            dma((2, by + bx + nx)),
            dma((6,)),
            pltpu.VMEM(queries.shape, queries.dtype),
            pltpu.VMEM(keys.shape, keys.dtype),
            pltpu.VMEM(values.shape, values.dtype),
            pltpu.VMEM(log_decay.shape, log_decay.dtype),
            pltpu.VMEM(level_weight.shape, level_weight.dtype),
        ],
        compiler_params=pltpu.CompilerParams(collective_id=0, has_side_effects=True, vmem_limit_bytes=40 * 2**20),
    )(*[pltpu.with_memory_space_constraint(v, pltpu.HBM) for v in (queries, keys, values, log_decay, level_weight, gain)])


def finish_kernel(acc_ref, lev_ref, right_ref, gain_ref, out_hbm, out_s, sems):
    heads, _, tokens = acc_ref.shape
    gain = gain_ref[...]
    sends = []
    for i in range(tokens // SPAN):
        at = slice(i * SPAN, (i + 1) * SPAN)
        for h in range(heads):
            mixed = acc_ref[h, :, at] + jnp.dot(lev_ref[h], right_ref[h, :, at], preferred_element_type=F32)
            square = jnp.mean(mixed * mixed, axis=0, keepdims=True)
            normed = (mixed * lax.rsqrt(square + 1e-05)).T
            out_s[at, h * 128 : (h + 1) * 128] = (normed * gain[:, h * 128 : (h + 1) * 128]).astype(BF16)
        send = pltpu.make_async_copy(out_s.at[at], out_hbm.at[at], sems.at[i])
        send.start()
        sends.append(send)
    for send in sends:
        send.wait()


def finish_part(acc, lev, right, gain):
    heads, _, tokens = acc.shape
    return pl.pallas_call(
        finish_kernel,
        out_shape=jax.ShapeDtypeStruct((tokens, heads * 128), BF16),
        in_specs=[VMEM] * 4,
        out_specs=pl.BlockSpec(memory_space=pl.ANY),
        scratch_shapes=[
            pltpu.VMEM((tokens, heads * 128), BF16),
            pltpu.SemaphoreType.DMA((tokens // SPAN,)),
        ],
        compiler_params=pltpu.CompilerParams(vmem_limit_bytes=24 * 2**20),
    )(acc, lev, right, gain)


def per_device(sizes, queries, keys, values, log_decay, level_weight, norm_gain):
    ny, nx, nz = sizes
    gain = norm_gain.reshape(1, -1)
    return finish_part(*main_part(ny, nx, nz, queries, keys, values, log_decay, level_weight, gain))


def solution(mesh, nx=4):
    sizes = (mesh.shape["narrow"] // 2, nx, mesh.shape["wide"] // nx)
    placed = (
        P(("wide", "narrow"), None),
        P(("wide", "narrow"), None),
        P(("wide", "narrow"), None),
        P(None, ("wide", "narrow")),
        P(None, None, ("wide", "narrow")),
        P(),
    )
    return jax.shard_map(
        functools.partial(per_device, sizes),
        mesh=mesh,
        in_specs=placed,
        out_specs=P(("wide", "narrow"), None),
        check_vma=False,
    )
```

```python
import functools

import jax
import jax.numpy as jnp
from jax import lax
from jax.experimental import pallas as pl
from jax.experimental.pallas import tpu as pltpu
from jax.sharding import PartitionSpec as P

MESH = pl.DeviceIdType.MESH
F32 = jnp.float32
BF16 = jnp.bfloat16
SPAN = 256
CHUNK = 128
VMEM = pl.BlockSpec(memory_space=pltpu.VMEM)


def lane(x, index):
    return jnp.broadcast_to(x[:, index : index + 1], x.shape)


def columns(index, width):
    return pl.ds(pl.multiple_of(index * width, width), width)


def far_first(n):
    return sorted(range(1, n), key=lambda o: -min(o, n - o))


def bits_of(n):
    return n.bit_length() - 1


def tree(states, fades):
    found = []
    states, fades = list(states), list(fades)
    while len(states) > 1:
        found.append(states[0::2])
        states = [states[i] * fades[i + 1] + states[i + 1] for i in range(0, len(states), 2)]
        fades = [fades[i] * fades[i + 1] for i in range(0, len(fades), 2)]
    return found, states[0]


def pick(items, index):
    out = items[0]
    for i in range(1, len(items)):
        out = jnp.where(index == i, items[i], out)
    return out


def prefixes(totals, index):
    out = []
    running = jnp.zeros_like(totals[0])
    for bit in range(bits_of(len(totals))):
        out.append(running)
        low = lax.rem(index, 2 ** (bit + 1))
        upper = low >= 2**bit
        start = index - low
        side = jnp.zeros_like(running)
        for i in range(len(totals)):
            inside = jnp.logical_and(i >= start, i < start + 2**bit)
            side = side + jnp.where(inside, totals[i], 0.0)
        running = running + jnp.where(upper, side, 0.0)
    return out, running


def main_kernel(
    ny, nx, nz, q_hbm, k_hbm, v_hbm, d_hbm, w_hbm, gain_hbm, acc_ref, lev_ref, right_ref, gain_ref,
    ext, mate_buf, chip_buf, r1, gq, gxq, gbuf, gx, hbuf, hz, lev, lvy, lvz, rights, span_s, half_s, rows_s, u_s, cum_ref, qt_ref, fade_s,
    e_sem, a_sem, p1_sem, p2_sem, g_sem, p3_sem, y_sem, x_sem, z_sem, f_sem, in_sem,
    q_ref, k_ref, v_ref, d_ref, w_ref,
):
    heads, tokens = d_ref.shape
    chunks, spans = tokens // CHUNK, tokens // SPAN
    local = bits_of(spans)
    by, bx, bz = bits_of(ny), bits_of(nx), bits_of(nz)
    first_x = 1 + by
    first_z = first_x + bx
    part = 128 // nx
    n = lax.axis_index("narrow")
    wide = lax.axis_index("wide")
    y, c = n // 2, lax.rem(n, 2)
    z, x = wide // nx, lax.rem(wide, nx)
    mate = n + 1 - 2 * c
    own_rows = pl.ds(pl.multiple_of(x * part, part), part)

    def copy(src, dst, sems, index, to_n, to_wide):
        return pltpu.make_async_remote_copy(
            src_ref=src, dst_ref=dst, send_sem=sems.at[0, index], recv_sem=sems.at[1, index],
            device_id={"narrow": to_n, "wide": to_wide}, device_id_type=MESH,
        )

    def has(index, bit):
        return lax.rem(index // 2**bit, 2) == 1

    fetches = [
        pltpu.make_async_copy(src, dst, in_sem.at[i])
        for i, (src, dst) in enumerate(
            [
                (d_hbm, d_ref), (k_hbm, k_ref), (v_hbm, v_ref), (q_hbm, q_ref), (w_hbm, w_ref),
                (gain_hbm, gain_ref),
            ]
        )
    ]
    for fetch in fetches:
        fetch.start()

    barrier = pltpu.get_barrier_semaphore()

    def hello(to_n, to_wide):
        pl.semaphore_signal(barrier, inc=1, device_id={"narrow": to_n, "wide": to_wide}, device_id_type=MESH)

    others = [(ox, oy) for ox in range(nx) for oy in range(ny) if ox or oy]
    others.sort(key=lambda o: -min(o[0], nx - o[0]) - min(o[1], ny - o[1]))
    for ox, oy in others:
        hello(lax.rem(y + oy, ny) * 2 + c, z * nx + lax.rem(x + ox, nx))
    for o in far_first(nz):

        @pl.when(z >= o)
        def _():
            hello(n, (z - o) * nx + x)

    hello(mate, wide)
    peers = len(others) + 1

    fetches[0].wait()
    at = [slice(m * CHUNK, (m + 1) * CHUNK) for m in range(chunks)]
    causal = lax.broadcasted_iota(jnp.int32, (CHUNK, CHUNK), 0) <= lax.broadcasted_iota(jnp.int32, (CHUNK, CHUNK), 1)
    stacked = jnp.concatenate([d_ref[:, at[m]] for m in range(chunks)], axis=0)
    sums = jnp.dot(stacked, causal.astype(F32), precision=lax.Precision.HIGHEST, preferred_element_type=F32)
    inside = [sums[m * heads : (m + 1) * heads] for m in range(chunks)]
    totals = [lane(v, CHUNK - 1) for v in inside]
    before = jnp.zeros_like(totals[0])
    for m in range(chunks):
        cum_ref[:, at[m]] = before + inside[m]
        before = before + totals[m]
    own_total = jnp.concatenate([before] * (8 // heads), axis=0)
    after = jnp.zeros_like(before)
    fades = [None] * chunks
    for m in reversed(range(chunks)):
        fades[m] = jnp.exp(after + (totals[m] - inside[m]))
        after = after + totals[m]

    fetches[1].wait()
    kt = k_ref[...].astype(F32).T
    for m in range(chunks):
        fade_s[:, at[m]] = fades[m]
    fetches[2].wait()

    def states(odd):
        for j in range(ny):
            h = 2 * j + odd
            keys = (kt * fade_s[pl.ds(h, 1), :]).astype(BF16)
            state = jnp.dot(keys, v_ref[:, columns(h, 128)], preferred_element_type=F32)
            ext[odd, j, :128] = state.T
            ext[odd, j, 128:] = own_total

    states(1 - c)
    pl.semaphore_wait(barrier, peers + nz - 1 - z)
    swap = copy(ext.at[1 - c], mate_buf, e_sem, 0, mate, wide)
    swap.start()
    states(c)
    level0 = copy(ext.at[:, :, pl.ds(0, 128)], lev.at[0], a_sem, 0, mate, wide)

    @pl.when(c == 0)
    def _():
        level0.start()

    @pl.when(c == 0)
    def _():
        lev[0] = jnp.zeros(lev.shape[1:], F32)

    swap.wait_recv()
    mate_total = mate_buf[0, 128:]
    for j in range(ny):
        mine = ext[c, j]
        theirs = mate_buf[j]
        row = pl.ds(128 + 2 * j + c, 1)
        left = jnp.where(c == 0, jnp.exp(mate_buf[j, row]), 1.0)
        right = jnp.where(c == 0, 1.0, jnp.exp(ext[c, j, row]))
        chip_buf[j, :128] = mine[:128] * left + theirs[:128] * right
        chip_buf[j, 128:] = mine[128:] + theirs[128:]

    def p1(o):
        to = lax.rem(y + o, ny)
        return copy(chip_buf.at[to], r1.at[y], p1_sem, o, to * 2 + c, wide)

    for o in far_first(ny):
        p1(o).start()

    fetches[3].wait()
    fetches[4].wait()
    fetches[5].wait()
    qt_ref[...] = q_ref[...].astype(F32).T
    for m in range(chunks):
        keys = k_ref[at[m], :]
        scores = jnp.dot(keys, qt_ref[:, at[m]].astype(BF16), preferred_element_type=F32)
        rights[m] = jnp.concatenate([jnp.where(causal, scores, 0.0).astype(BF16), keys], axis=1)
        middle = lane(inside[m], CHUNK // 2 - 1)
        rows_s[0, :, at[m]] = jnp.exp(middle - inside[m])
        rows_s[1, :, at[m]] = w_ref[0, :, at[m]] * jnp.exp(inside[m] - middle)
        rows_s[2, :, at[m]] = jnp.exp(totals[m] - middle)
        rows_s[3, :, at[m]] = jnp.exp(totals[m])
    span_total = [totals[2 * i] + totals[2 * i + 1] for i in range(spans)]
    for m in range(chunks):
        inner = inside[m] + totals[m - 1] if m % 2 == 1 else inside[m]
        u_s[0, :, at[m]] = w_ref[0, :, at[m]] * jnp.exp(inside[m]) if m % 2 == 1 else jnp.zeros_like(inner)
        u_s[1, :, at[m]] = w_ref[1, :, at[m]] * jnp.exp(inner)
        u_s[2, :, at[m]] = w_ref[2, :, at[m]] * jnp.exp(inner + span_total[2] if m // 2 == 3 else inner)

    def chunk_products(h, carry):
        one = pl.ds(h, 1)
        out_row, in_row, rest_row, whole_row = [rows_s[i, one, :] for i in range(4)]
        for m in range(chunks):
            vt = v_ref[at[m], columns(h, 128)].T.astype(F32)
            left = (vt * out_row[:, at[m]]).astype(BF16)
            out = jnp.dot(left, rights[m], preferred_element_type=F32)
            acc_ref[h, :, at[m]] = out[:, :CHUNK] * in_row[:, at[m]]
            state = out[:, CHUNK:] * rest_row[:, at[m]]
            if m % 2 == 0:
                half_s[m // 2, h] = state
            else:
                span_s[m // 2, h] = half_s[m // 2, h] * whole_row[:, at[m]] + state
        return carry

    lax.fori_loop(0, heads, chunk_products, 0)

    r1[y] = chip_buf[y]
    for o in range(1, ny):
        source = lax.rem(y + ny - o, ny)
        copy(r1.at[source], r1.at[source], p1_sem, o, n, wide).wait_recv()
    chip_totals = [r1[i, 128:] for i in range(ny)]
    found, group = tree([r1[i, :128] for i in range(ny)], [jnp.exp(r1[i, pl.ds(128 + n, 1)]) for i in range(ny)])
    group_total = chip_totals[0]
    for i in range(1, ny):
        group_total = group_total + chip_totals[i]
    for i in range(nx):
        gq[i, :part] = group[i * part : (i + 1) * part]
        gq[i, part:] = group_total
    gbuf[...] = group

    def p2(o):
        to = lax.rem(x + o, nx)
        return copy(gq.at[to], gxq.at[x], p2_sem, o, n, z * nx + to)

    def x_send(bit, src, oy, to_x):
        return copy(
            src, lev.at[first_x + bit, c, y], x_sem, bit * ny + oy,
            lax.rem(y + oy, ny) * 2 + c, z * nx + to_x,
        )

    def x_arrived(bit, oy):
        block = lev.at[first_x + bit, c, lax.rem(y + ny - oy, ny)]
        copy(block, block, x_sem, bit * ny + oy, n, wide).wait_recv()

    def to_row_before():
        return copy(gbuf, gx.at[0], g_sem, 0, n, wide - 1)

    for o in far_first(nx):
        p2(o).start()

    slot = 0
    slots = []
    for bit in range(by):
        slots.append(slot)
        for item in found[bit]:
            lvy[slot] = item
            slot += 1

    def y_copy(bit, o):
        to = lax.rem(y + o, ny)
        return copy(
            lvy.at[slots[bit] + to // 2 ** (bit + 1)], lev.at[1 + bit, c, y], y_sem, bit * ny + o, to * 2 + c, wide
        )

    for bit in range(by):
        for o in range(1, ny):

            @pl.when(has(lax.rem(y + o, ny), bit))
            def _():
                y_copy(bit, o).start()

        @pl.when(has(y, bit))
        def _():
            lev[1 + bit, c, y] = lvy[slots[bit] + y // 2 ** (bit + 1)]

        @pl.when(jnp.logical_not(has(y, bit)))
        def _():
            lev[1 + bit] = jnp.zeros(lev.shape[1:], F32)

    gxq[x] = gq[x]
    for o in range(1, nx):
        source = lax.rem(x + nx - o, nx)
        copy(gxq.at[source], gxq.at[source], p2_sem, o, n, wide).wait_recv()
    x_totals = [gxq[i, part:] for i in range(nx)]
    x_fades = [jnp.exp(gxq[i, pl.ds(part + n, 1)]) for i in range(nx)]
    _, plane = tree([gxq[i, :part] for i in range(nx)], x_fades)
    plane_total = x_totals[0]
    for i in range(1, nx):
        plane_total = plane_total + x_totals[i]
    hbuf[:part] = plane
    hbuf[part:] = plane_total

    def p3(o):
        return copy(hbuf, hz.at[z], p3_sem, o, n, (z + o) * nx + x)

    for o in far_first(nz):

        @pl.when(z + o < nz)
        def _():
            p3(o).start()

    if bx > 1:

        @pl.when(x == 1)
        def _():
            to_row_before().start()

    @pl.when(jnp.logical_not(has(x, 0)))
    def _():
        for oy in range(ny):
            x_send(0, gbuf, oy, x + 1).start()
        lev[first_x] = jnp.zeros(lev.shape[1:], F32)

    @pl.when(has(x, 0))
    def _():
        x_arrived(0, 0)

    if bx > 1:

        @pl.when(x == 1)
        def _():
            gx[1] = lev[first_x, c, y] * x_fades[1] + gbuf[...]
            for oy in range(ny):
                x_send(1, gx.at[1], oy, 2).start()

        @pl.when(x == 0)
        def _():
            copy(gx.at[0], gx.at[0], g_sem, 0, n, wide).wait_recv()
            gx[1] = gbuf[...] * x_fades[1] + gx[0]
            for oy in range(ny):
                x_send(1, gx.at[1], oy, 3).start()

        @pl.when(jnp.logical_not(has(x, 1)))
        def _():
            lev[first_x + 1] = jnp.zeros(lev.shape[1:], F32)

    def forward(first, count, index):
        block = lev.at[pl.ds(first, count), c]
        return copy(block, block, f_sem, index, mate, wide)

    def forwarded(first, count, index):
        block = lev.at[pl.ds(first, count), 1 - c]
        return copy(block, block, f_sem, index, mate, wide)

    for bit in range(by):

        @pl.when(has(y, bit))
        def _():
            for o in range(1, ny):
                source = lax.rem(y + ny - o, ny)
                block = lev.at[1 + bit, c, source]
                copy(block, block, y_sem, bit * ny + o, n, wide).wait_recv()
            forward(1 + bit, 1, bit).start()

    def z_block(count, from_y, from_x):
        rows = pl.ds(pl.multiple_of(from_x * part, part), part)
        return lev.at[pl.ds(first_z, count), c, from_y, rows]

    def z_copy(count, ox, oy):
        return copy(
            lvz.at[pl.ds(0, count)], z_block(count, y, x), z_sem, ox * ny + oy,
            lax.rem(y + oy, ny) * 2 + c, z * nx + lax.rem(x + ox, nx),
        )

    def z_forward(count, parity, ox):
        rows = pl.ds(pl.multiple_of(lax.rem(x + nx - ox, nx) * part, part), part)
        block = lev.at[pl.ds(first_z, count), parity, :, rows]
        return copy(block, block, f_sem, by + bx + ox, mate, wide)

    near = sorted(range(nx), key=lambda o: min(o, nx - o))
    slot_of = [sum([lax.rem(z // 2**i, 2) for i in range(bit)], z * 0) for bit in range(bz)]
    held = sum([lax.rem(z // 2**i, 2) for i in range(bz)], z * 0)
    for o in range(1, nz):

        @pl.when(z >= o)
        def _():
            copy(hz.at[z - o], hz.at[z - o], p3_sem, o, n, wide).wait_recv()

    z_totals = [hz[i, part:] for i in range(nz)]
    found, _ = tree([hz[i, :part] for i in range(nz)], [jnp.exp(hz[i, pl.ds(part + n, 1)]) for i in range(nz)])
    for bit in range(bz):

        @pl.when(has(z, bit))
        def _():
            lvz[slot_of[bit]] = pick(found[bit], z // 2 ** (bit + 1))

    for count in range(1, bz + 1):

        @pl.when(held == count)
        def _():
            for ox, oy in others:
                z_copy(count, ox, oy).start()
            lev[first_z : first_z + count, c, y, own_rows] = lvz[:count]

    for slot in range(bz):

        @pl.when(held <= slot)
        def _():
            lev[first_z + slot] = jnp.zeros(lev.shape[1:], F32)

    def local_levels(h, carry):
        one = pl.ds(h, 1)
        whole_row = rows_s[3, one, :]
        scales = [u_s[level, one, :] for level in range(3)]
        first = span_s[0, h]
        pair = first * (whole_row[:, at[2]] * whole_row[:, at[3]]) + span_s[1, h]
        parts = [[], [(1, first)], [(2, pair)], [(1, span_s[2, h]), (2, pair)]]
        for i in range(spans):
            here = slice(i * SPAN, (i + 1) * SPAN)
            items = [(0, half_s[i, h])] + parts[i]
            left = jnp.concatenate([v.astype(BF16) for _, v in items], axis=1)
            right = jnp.concatenate(
                [(qt_ref[:, here] * scales[level][:, here]).astype(BF16) for level, _ in items], axis=0
            )
            acc_ref[h, :, here] += jnp.dot(left, right, preferred_element_type=F32)
        return carry

    low = jnp.where(c == 1, mate_total, 0.0)
    chip_pre, y_running = prefixes(chip_totals, y)
    middle, x_running = prefixes(x_totals, x)
    high, _ = prefixes(z_totals, z)
    base = low + y_running
    pres = [jnp.zeros_like(low)] + [low + v for v in chip_pre]
    pres += [base + v for v in middle] + [base + x_running + v for v in high]

    def scale(level):
        wide_pre = jnp.concatenate([pres[level][:heads]] * chunks, axis=1)
        return w_ref[1 + local + level] * jnp.exp(cum_ref[...] + wide_pre)

    for level in range(first_z):
        u_s[1 + local + level] = scale(level)
    for bit in range(bz):
        u_s[1 + local + first_z + bit] = jnp.zeros((heads, tokens), F32)
    for bit in range(bz):

        @pl.when(has(z, bit))
        def _():
            u_s[1 + local + first_z + slot_of[bit]] = scale(first_z + bit)

    def z_rights(h, carry):
        one = pl.ds(h, 1)
        for slot in range(bz):
            row = u_s[1 + local + first_z + slot, one, :]
            right_ref[h, slot * 128 : (slot + 1) * 128, :] = (qt_ref[...] * row).astype(BF16)
        return carry

    def level_products(levels):
        def body(h, carry):
            one = pl.ds(h, 1)
            left = jnp.concatenate([lev[level, lax.rem(h, 2), h // 2].astype(BF16) for level in levels], axis=1)
            scales = [u_s[1 + local + level, one, :] for level in levels]
            for i in range(spans):
                here = slice(i * SPAN, (i + 1) * SPAN)
                right = jnp.concatenate([(qt_ref[:, here] * row[:, here]).astype(BF16) for row in scales], axis=0)
                acc_ref[h, :, here] += jnp.dot(left, right, preferred_element_type=F32)
            return carry

        lax.fori_loop(0, heads, body, 0)

    lax.fori_loop(0, heads, z_rights, 0)
    lax.fori_loop(0, heads, local_levels, 0)
    for bit in range(by):

        @pl.when(has(y, bit))
        def _():
            forwarded(1 + bit, 1, bit).wait_recv()

    @pl.when(c == 1)
    def _():
        level0.wait_recv()

    level_products(range(first_x))

    for bit in range(bx):

        @pl.when(has(x, bit))
        def _():
            for oy in range(1 if bit == 0 else 0, ny):
                x_arrived(bit, oy)
            forward(first_x + bit, 1, by + bit).start()

    for count in range(1, bz + 1):

        @pl.when(held == count)
        def _():
            for ox in near:
                for oy in range(ny):
                    if ox or oy:
                        block = z_block(count, lax.rem(y + ny - oy, ny), lax.rem(x + nx - ox, nx))
                        copy(block, block, z_sem, ox * ny + oy, n, wide).wait_recv()
                z_forward(count, c, ox).start()

    for bit in range(bx):

        @pl.when(has(x, bit))
        def _():
            forwarded(first_x + bit, 1, by + bit).wait_recv()

    level_products(range(first_x, first_z))

    swap.wait_send()

    @pl.when(c == 0)
    def _():
        level0.wait_send()

    for o in range(1, ny):
        p1(o).wait_send()
    for o in range(1, nx):
        p2(o).wait_send()
    for o in range(1, nz):

        @pl.when(z + o < nz)
        def _():
            p3(o).wait_send()

    for bit in range(bx):

        @pl.when(has(x, bit))
        def _():
            forward(first_x + bit, 1, by + bit).wait_send()

    @pl.when(jnp.logical_not(has(x, 0)))
    def _():
        for oy in range(ny):
            x_send(0, gbuf, oy, x + 1).wait_send()

    if bx > 1:

        @pl.when(x == 1)
        def _():
            to_row_before().wait_send()
            for oy in range(ny):
                x_send(1, gx.at[1], oy, 2).wait_send()

        @pl.when(x == 0)
        def _():
            for oy in range(ny):
                x_send(1, gx.at[1], oy, 3).wait_send()

    for bit in range(by):
        for o in range(1, ny):

            @pl.when(has(lax.rem(y + o, ny), bit))
            def _():
                y_copy(bit, o).wait_send()

        @pl.when(has(y, bit))
        def _():
            forward(1 + bit, 1, bit).wait_send()

    for count in range(1, bz + 1):

        @pl.when(held == count)
        def _():
            for ox, oy in others:
                z_copy(count, ox, oy).wait_send()
            for ox in near:
                z_forward(count, 1 - c, ox).wait_recv()
            for ox in near:
                z_forward(count, c, ox).wait_send()

    for slot in range(bz):
        for h in range(heads):
            lev_ref[h, :, slot * 128 : (slot + 1) * 128] = lev[first_z + slot, h % 2, h // 2].astype(BF16)


def main_part(ny, nx, nz, queries, keys, values, log_decay, level_weight, gain):
    heads, tokens = log_decay.shape
    by, bx, bz = bits_of(ny), bits_of(nx), bits_of(nz)
    levels = 1 + by + bx + bz
    chunks, spans = tokens // CHUNK, tokens // SPAN
    part = 128 // nx
    dma = pltpu.SemaphoreType.DMA
    return pl.pallas_call(
        functools.partial(main_kernel, ny, nx, nz),
        out_shape=(
            jax.ShapeDtypeStruct((heads, 128, tokens), F32),
            jax.ShapeDtypeStruct((heads, 128, bz * 128), BF16),
            jax.ShapeDtypeStruct((heads, bz * 128, tokens), BF16),
            jax.ShapeDtypeStruct(gain.shape, F32),
        ),
        in_specs=[pl.BlockSpec(memory_space=pltpu.HBM)] * 6,
        out_specs=(VMEM,) * 4,
        scratch_shapes=[
            pltpu.VMEM((2, ny, 136, 128), F32),
            pltpu.VMEM((ny, 136, 128), F32),
            pltpu.VMEM((ny, 136, 128), F32),
            pltpu.VMEM((ny, 136, 128), F32),
            pltpu.VMEM((nx, part + 8, 128), F32),
            pltpu.VMEM((nx, part + 8, 128), F32),
            pltpu.VMEM((128, 128), F32),
            pltpu.VMEM((2, 128, 128), F32),
            pltpu.VMEM((part + 8, 128), F32),
            pltpu.VMEM((nz, part + 8, 128), F32),
            pltpu.VMEM((levels, 2, ny, 128, 128), F32),
            pltpu.VMEM((ny, 128, 128), F32),
            pltpu.VMEM((bz, part, 128), F32),
            pltpu.VMEM((chunks, CHUNK, 2 * CHUNK), BF16),
            pltpu.VMEM((spans, heads, 128, 128), F32),
            pltpu.VMEM((spans, heads, 128, 128), F32),
            pltpu.VMEM((4, heads, tokens), F32),
            pltpu.VMEM((1 + bits_of(spans) + levels, heads, tokens), F32),
            pltpu.VMEM((heads, tokens), F32),
            pltpu.VMEM((128, tokens), F32),
            pltpu.VMEM((heads, tokens), F32),
            dma((2, 1)),
            dma((2, 1)),
            dma((2, ny)),
            dma((2, nx)),
            dma((2, 1)),
            dma((2, nz)),
            dma((2, by * ny)),
            dma((2, bx * ny)),
            dma((2, nx * ny)),
            dma((2, by + bx + nx)),
            dma((6,)),
            pltpu.VMEM(queries.shape, queries.dtype),
            pltpu.VMEM(keys.shape, keys.dtype),
            pltpu.VMEM(values.shape, values.dtype),
            pltpu.VMEM(log_decay.shape, log_decay.dtype),
            pltpu.VMEM(level_weight.shape, level_weight.dtype),
        ],
        compiler_params=pltpu.CompilerParams(collective_id=0, has_side_effects=True, vmem_limit_bytes=40 * 2**20),
    )(*[pltpu.with_memory_space_constraint(v, pltpu.HBM) for v in (queries, keys, values, log_decay, level_weight, gain)])


def finish_kernel(acc_ref, lev_ref, right_ref, gain_ref, out_hbm, out_s, sems):
    heads, _, tokens = acc_ref.shape
    gain = gain_ref[...]
    sends = []
    for i in range(tokens // SPAN):
        at = slice(i * SPAN, (i + 1) * SPAN)
        for h in range(heads):
            mixed = acc_ref[h, :, at] + jnp.dot(lev_ref[h], right_ref[h, :, at], preferred_element_type=F32)
            square = jnp.mean(mixed * mixed, axis=0, keepdims=True)
            normed = (mixed * lax.rsqrt(square + 1e-05)).T
            out_s[at, h * 128 : (h + 1) * 128] = (normed * gain[:, h * 128 : (h + 1) * 128]).astype(BF16)
        send = pltpu.make_async_copy(out_s.at[at], out_hbm.at[at], sems.at[i])
        send.start()
        sends.append(send)
    for send in sends:
        send.wait()


def finish_part(acc, lev, right, gain):
    heads, _, tokens = acc.shape
    return pl.pallas_call(
        finish_kernel,
        out_shape=jax.ShapeDtypeStruct((tokens, heads * 128), BF16),
        in_specs=[VMEM] * 4,
        out_specs=pl.BlockSpec(memory_space=pl.ANY),
        scratch_shapes=[
            pltpu.VMEM((tokens, heads * 128), BF16),
            pltpu.SemaphoreType.DMA((tokens // SPAN,)),
        ],
        compiler_params=pltpu.CompilerParams(vmem_limit_bytes=24 * 2**20),
    )(acc, lev, right, gain)


def per_device(sizes, queries, keys, values, log_decay, level_weight, norm_gain):
    ny, nx, nz = sizes
    gain = norm_gain.reshape(1, -1)
    return finish_part(*main_part(ny, nx, nz, queries, keys, values, log_decay, level_weight, gain))


def solution(mesh, nx=4):
    sizes = (mesh.shape["narrow"] // 2, nx, mesh.shape["wide"] // nx)
    placed = (
        P(("wide", "narrow"), None),
        P(("wide", "narrow"), None),
        P(("wide", "narrow"), None),
        P(None, ("wide", "narrow")),
        P(None, None, ("wide", "narrow")),
        P(),
    )
    return jax.shard_map(
        functools.partial(per_device, sizes),
        mesh=mesh,
        in_specs=placed,
        out_specs=P(("wide", "narrow"), None),
        check_vma=False,
    )
```

```python
import functools

import jax
import jax.numpy as jnp
from jax import lax
from jax.experimental import pallas as pl
from jax.experimental.pallas import tpu as pltpu
from jax.sharding import PartitionSpec as P

MESH = pl.DeviceIdType.MESH
F32 = jnp.float32
BF16 = jnp.bfloat16
SPAN = 256
CHUNK = 128
VMEM = pl.BlockSpec(memory_space=pltpu.VMEM)


def lane(x, index):
    return jnp.broadcast_to(x[:, index : index + 1], x.shape)


def columns(index, width):
    return pl.ds(pl.multiple_of(index * width, width), width)


def far_first(n):
    return sorted(range(1, n), key=lambda o: -min(o, n - o))


def bits_of(n):
    return n.bit_length() - 1


def tree(states, fades):
    found = []
    states, fades = list(states), list(fades)
    while len(states) > 1:
        found.append(states[0::2])
        states = [states[i] * fades[i + 1] + states[i + 1] for i in range(0, len(states), 2)]
        fades = [fades[i] * fades[i + 1] for i in range(0, len(fades), 2)]
    return found, states[0]


def pick(items, index):
    out = items[0]
    for i in range(1, len(items)):
        out = jnp.where(index == i, items[i], out)
    return out


def prefixes(totals, index):
    out = []
    running = jnp.zeros_like(totals[0])
    for bit in range(bits_of(len(totals))):
        out.append(running)
        low = lax.rem(index, 2 ** (bit + 1))
        upper = low >= 2**bit
        start = index - low
        side = jnp.zeros_like(running)
        for i in range(len(totals)):
            inside = jnp.logical_and(i >= start, i < start + 2**bit)
            side = side + jnp.where(inside, totals[i], 0.0)
        running = running + jnp.where(upper, side, 0.0)
    return out, running


def main_kernel(
    ny, nx, nz, q_hbm, k_hbm, v_hbm, d_hbm, w_hbm, gain_hbm, acc_ref, lev_ref, right_ref, gain_ref,
    ext, mate_buf, chip_buf, r1, gq, gxq, gbuf, gx, hbuf, hz, lev, lvy, lvz, rights, span_s, half_s, rows_s, u_s, cum_ref, qt_ref, fade_s,
    e_sem, a_sem, p1_sem, p2_sem, g_sem, p3_sem, y_sem, x_sem, z_sem, f_sem, in_sem,
    q_ref, k_ref, v_ref, d_ref, w_ref,
):
    heads, tokens = d_ref.shape
    chunks, spans = tokens // CHUNK, tokens // SPAN
    local = bits_of(spans)
    by, bx, bz = bits_of(ny), bits_of(nx), bits_of(nz)
    first_x = 1 + by
    first_z = first_x + bx
    part = 128 // nx
    n = lax.axis_index("narrow")
    wide = lax.axis_index("wide")
    y, c = n // 2, lax.rem(n, 2)
    z, x = wide // nx, lax.rem(wide, nx)
    mate = n + 1 - 2 * c
    own_rows = pl.ds(pl.multiple_of(x * part, part), part)

    def copy(src, dst, sems, index, to_n, to_wide):
        return pltpu.make_async_remote_copy(
            src_ref=src, dst_ref=dst, send_sem=sems.at[0, index], recv_sem=sems.at[1, index],
            device_id={"narrow": to_n, "wide": to_wide}, device_id_type=MESH,
        )

    def has(index, bit):
        return lax.rem(index // 2**bit, 2) == 1

    fetches = [
        pltpu.make_async_copy(src, dst, in_sem.at[i])
        for i, (src, dst) in enumerate(
            [
                (d_hbm, d_ref), (k_hbm, k_ref), (v_hbm, v_ref), (q_hbm, q_ref), (w_hbm, w_ref),
                (gain_hbm, gain_ref),
            ]
        )
    ]
    for fetch in fetches:
        fetch.start()

    barrier = pltpu.get_barrier_semaphore()

    def hello(to_n, to_wide):
        pl.semaphore_signal(barrier, inc=1, device_id={"narrow": to_n, "wide": to_wide}, device_id_type=MESH)

    others = [(ox, oy) for ox in range(nx) for oy in range(ny) if ox or oy]
    others.sort(key=lambda o: -min(o[0], nx - o[0]) - min(o[1], ny - o[1]))
    for ox, oy in others:
        hello(lax.rem(y + oy, ny) * 2 + c, z * nx + lax.rem(x + ox, nx))
    for o in far_first(nz):

        @pl.when(z >= o)
        def _():
            hello(n, (z - o) * nx + x)

    hello(mate, wide)
    peers = len(others) + 1

    fetches[0].wait()
    at = [slice(m * CHUNK, (m + 1) * CHUNK) for m in range(chunks)]
    causal = lax.broadcasted_iota(jnp.int32, (CHUNK, CHUNK), 0) <= lax.broadcasted_iota(jnp.int32, (CHUNK, CHUNK), 1)
    stacked = jnp.concatenate([d_ref[:, at[m]] for m in range(chunks)], axis=0)
    sums = jnp.dot(stacked, causal.astype(F32), precision=lax.Precision.HIGHEST, preferred_element_type=F32)
    inside = [sums[m * heads : (m + 1) * heads] for m in range(chunks)]
    totals = [lane(v, CHUNK - 1) for v in inside]
    before = jnp.zeros_like(totals[0])
    for m in range(chunks):
        cum_ref[:, at[m]] = before + inside[m]
        before = before + totals[m]
    own_total = jnp.concatenate([before] * (8 // heads), axis=0)
    after = jnp.zeros_like(before)
    fades = [None] * chunks
    for m in reversed(range(chunks)):
        fades[m] = jnp.exp(after + (totals[m] - inside[m]))
        after = after + totals[m]

    fetches[1].wait()
    kt = k_ref[...].astype(F32).T
    for m in range(chunks):
        fade_s[:, at[m]] = fades[m]
    fetches[2].wait()

    def states(odd):
        for j in range(ny):
            h = 2 * j + odd
            keys = (kt * fade_s[pl.ds(h, 1), :]).astype(BF16)
            state = jnp.dot(keys, v_ref[:, columns(h, 128)], preferred_element_type=F32)
            ext[odd, j, :128] = state.T
            ext[odd, j, 128:] = own_total

    states(1 - c)
    pl.semaphore_wait(barrier, peers + nz - 1 - z)
    swap = copy(ext.at[1 - c], mate_buf, e_sem, 0, mate, wide)
    swap.start()
    states(c)
    level0 = copy(ext.at[:, :, pl.ds(0, 128)], lev.at[0], a_sem, 0, mate, wide)

    @pl.when(c == 0)
    def _():
        lev[0] = jnp.zeros(lev.shape[1:], F32)

    swap.wait_recv()
    mate_total = mate_buf[0, 128:]
    for j in range(ny):
        mine = ext[c, j]
        theirs = mate_buf[j]
        row = pl.ds(128 + 2 * j + c, 1)
        left = jnp.where(c == 0, jnp.exp(mate_buf[j, row]), 1.0)
        right = jnp.where(c == 0, 1.0, jnp.exp(ext[c, j, row]))
        chip_buf[j, :128] = mine[:128] * left + theirs[:128] * right
        chip_buf[j, 128:] = mine[128:] + theirs[128:]

    def p1(o):
        to = lax.rem(y + o, ny)
        return copy(chip_buf.at[to], r1.at[y], p1_sem, o, to * 2 + c, wide)

    for o in far_first(ny):
        p1(o).start()

    @pl.when(c == 0)
    def _():
        level0.start()

    fetches[3].wait()
    fetches[4].wait()
    fetches[5].wait()
    qt_ref[...] = q_ref[...].astype(F32).T
    for m in range(chunks):
        keys = k_ref[at[m], :]
        scores = jnp.dot(keys, qt_ref[:, at[m]].astype(BF16), preferred_element_type=F32)
        rights[m] = jnp.concatenate([jnp.where(causal, scores, 0.0).astype(BF16), keys], axis=1)
        middle = lane(inside[m], CHUNK // 2 - 1)
        rows_s[0, :, at[m]] = jnp.exp(middle - inside[m])
        rows_s[1, :, at[m]] = w_ref[0, :, at[m]] * jnp.exp(inside[m] - middle)
        rows_s[2, :, at[m]] = jnp.exp(totals[m] - middle)
        rows_s[3, :, at[m]] = jnp.exp(totals[m])
    span_total = [totals[2 * i] + totals[2 * i + 1] for i in range(spans)]
    for m in range(chunks):
        inner = inside[m] + totals[m - 1] if m % 2 == 1 else inside[m]
        u_s[0, :, at[m]] = w_ref[0, :, at[m]] * jnp.exp(inside[m]) if m % 2 == 1 else jnp.zeros_like(inner)
        u_s[1, :, at[m]] = w_ref[1, :, at[m]] * jnp.exp(inner)
        u_s[2, :, at[m]] = w_ref[2, :, at[m]] * jnp.exp(inner + span_total[2] if m // 2 == 3 else inner)

    def chunk_products(h, carry):
        one = pl.ds(h, 1)
        out_row, in_row, rest_row, whole_row = [rows_s[i, one, :] for i in range(4)]
        for m in range(chunks):
            vt = v_ref[at[m], columns(h, 128)].T.astype(F32)
            left = (vt * out_row[:, at[m]]).astype(BF16)
            out = jnp.dot(left, rights[m], preferred_element_type=F32)
            acc_ref[h, :, at[m]] = out[:, :CHUNK] * in_row[:, at[m]]
            state = out[:, CHUNK:] * rest_row[:, at[m]]
            if m % 2 == 0:
                half_s[m // 2, h] = state
            else:
                span_s[m // 2, h] = half_s[m // 2, h] * whole_row[:, at[m]] + state
        return carry

    lax.fori_loop(0, heads, chunk_products, 0)

    r1[y] = chip_buf[y]
    for o in range(1, ny):
        source = lax.rem(y + ny - o, ny)
        copy(r1.at[source], r1.at[source], p1_sem, o, n, wide).wait_recv()
    chip_totals = [r1[i, 128:] for i in range(ny)]
    found, group = tree([r1[i, :128] for i in range(ny)], [jnp.exp(r1[i, pl.ds(128 + n, 1)]) for i in range(ny)])
    group_total = chip_totals[0]
    for i in range(1, ny):
        group_total = group_total + chip_totals[i]
    for i in range(nx):
        gq[i, :part] = group[i * part : (i + 1) * part]
        gq[i, part:] = group_total
    gbuf[...] = group

    def p2(o):
        to = lax.rem(x + o, nx)
        return copy(gq.at[to], gxq.at[x], p2_sem, o, n, z * nx + to)

    def x_send(bit, src, oy, to_x):
        return copy(
            src, lev.at[first_x + bit, c, y], x_sem, bit * ny + oy,
            lax.rem(y + oy, ny) * 2 + c, z * nx + to_x,
        )

    def x_arrived(bit, oy):
        block = lev.at[first_x + bit, c, lax.rem(y + ny - oy, ny)]
        copy(block, block, x_sem, bit * ny + oy, n, wide).wait_recv()

    def to_row_before():
        return copy(gbuf, gx.at[0], g_sem, 0, n, wide - 1)

    for o in far_first(nx):
        p2(o).start()

    slot = 0
    slots = []
    for bit in range(by):
        slots.append(slot)
        for item in found[bit]:
            lvy[slot] = item
            slot += 1

    def y_copy(bit, o):
        to = lax.rem(y + o, ny)
        return copy(
            lvy.at[slots[bit] + to // 2 ** (bit + 1)], lev.at[1 + bit, c, y], y_sem, bit * ny + o, to * 2 + c, wide
        )

    for bit in range(by):
        for o in range(1, ny):

            @pl.when(has(lax.rem(y + o, ny), bit))
            def _():
                y_copy(bit, o).start()

        @pl.when(has(y, bit))
        def _():
            lev[1 + bit, c, y] = lvy[slots[bit] + y // 2 ** (bit + 1)]

        @pl.when(jnp.logical_not(has(y, bit)))
        def _():
            lev[1 + bit] = jnp.zeros(lev.shape[1:], F32)

    gxq[x] = gq[x]
    for o in range(1, nx):
        source = lax.rem(x + nx - o, nx)
        copy(gxq.at[source], gxq.at[source], p2_sem, o, n, wide).wait_recv()
    x_totals = [gxq[i, part:] for i in range(nx)]
    x_fades = [jnp.exp(gxq[i, pl.ds(part + n, 1)]) for i in range(nx)]
    _, plane = tree([gxq[i, :part] for i in range(nx)], x_fades)
    plane_total = x_totals[0]
    for i in range(1, nx):
        plane_total = plane_total + x_totals[i]
    hbuf[:part] = plane
    hbuf[part:] = plane_total

    def p3(o):
        return copy(hbuf, hz.at[z], p3_sem, o, n, (z + o) * nx + x)

    for o in far_first(nz):

        @pl.when(z + o < nz)
        def _():
            p3(o).start()

    if bx > 1:

        @pl.when(x == 1)
        def _():
            to_row_before().start()

    @pl.when(jnp.logical_not(has(x, 0)))
    def _():
        for oy in range(ny):
            x_send(0, gbuf, oy, x + 1).start()
        lev[first_x] = jnp.zeros(lev.shape[1:], F32)

    @pl.when(has(x, 0))
    def _():
        x_arrived(0, 0)

    if bx > 1:

        @pl.when(x == 1)
        def _():
            gx[1] = lev[first_x, c, y] * x_fades[1] + gbuf[...]
            for oy in range(ny):
                x_send(1, gx.at[1], oy, 2).start()

        @pl.when(x == 0)
        def _():
            copy(gx.at[0], gx.at[0], g_sem, 0, n, wide).wait_recv()
            gx[1] = gbuf[...] * x_fades[1] + gx[0]
            for oy in range(ny):
                x_send(1, gx.at[1], oy, 3).start()

        @pl.when(jnp.logical_not(has(x, 1)))
        def _():
            lev[first_x + 1] = jnp.zeros(lev.shape[1:], F32)

    def forward(first, count, index):
        block = lev.at[pl.ds(first, count), c]
        return copy(block, block, f_sem, index, mate, wide)

    def forwarded(first, count, index):
        block = lev.at[pl.ds(first, count), 1 - c]
        return copy(block, block, f_sem, index, mate, wide)

    for bit in range(by):

        @pl.when(has(y, bit))
        def _():
            for o in range(1, ny):
                source = lax.rem(y + ny - o, ny)
                block = lev.at[1 + bit, c, source]
                copy(block, block, y_sem, bit * ny + o, n, wide).wait_recv()
            forward(1 + bit, 1, bit).start()

    def z_block(count, from_y, from_x):
        rows = pl.ds(pl.multiple_of(from_x * part, part), part)
        return lev.at[pl.ds(first_z, count), c, from_y, rows]

    def z_copy(count, ox, oy):
        return copy(
            lvz.at[pl.ds(0, count)], z_block(count, y, x), z_sem, ox * ny + oy,
            lax.rem(y + oy, ny) * 2 + c, z * nx + lax.rem(x + ox, nx),
        )

    def z_forward(count, parity, ox):
        rows = pl.ds(pl.multiple_of(lax.rem(x + nx - ox, nx) * part, part), part)
        block = lev.at[pl.ds(first_z, count), parity, :, rows]
        return copy(block, block, f_sem, by + bx + ox, mate, wide)

    near = sorted(range(nx), key=lambda o: min(o, nx - o))
    slot_of = [sum([lax.rem(z // 2**i, 2) for i in range(bit)], z * 0) for bit in range(bz)]
    held = sum([lax.rem(z // 2**i, 2) for i in range(bz)], z * 0)
    for o in range(1, nz):

        @pl.when(z >= o)
        def _():
            copy(hz.at[z - o], hz.at[z - o], p3_sem, o, n, wide).wait_recv()

    z_totals = [hz[i, part:] for i in range(nz)]
    found, _ = tree([hz[i, :part] for i in range(nz)], [jnp.exp(hz[i, pl.ds(part + n, 1)]) for i in range(nz)])
    for bit in range(bz):

        @pl.when(has(z, bit))
        def _():
            lvz[slot_of[bit]] = pick(found[bit], z // 2 ** (bit + 1))

    for count in range(1, bz + 1):

        @pl.when(held == count)
        def _():
            for ox, oy in others:
                z_copy(count, ox, oy).start()
            lev[first_z : first_z + count, c, y, own_rows] = lvz[:count]

    for slot in range(bz):

        @pl.when(held <= slot)
        def _():
            lev[first_z + slot] = jnp.zeros(lev.shape[1:], F32)

    def local_levels(h, carry):
        one = pl.ds(h, 1)
        whole_row = rows_s[3, one, :]
        scales = [u_s[level, one, :] for level in range(3)]
        first = span_s[0, h]
        pair = first * (whole_row[:, at[2]] * whole_row[:, at[3]]) + span_s[1, h]
        parts = [[], [(1, first)], [(2, pair)], [(1, span_s[2, h]), (2, pair)]]
        for i in range(spans):
            here = slice(i * SPAN, (i + 1) * SPAN)
            items = [(0, half_s[i, h])] + parts[i]
            left = jnp.concatenate([v.astype(BF16) for _, v in items], axis=1)
            right = jnp.concatenate(
                [(qt_ref[:, here] * scales[level][:, here]).astype(BF16) for level, _ in items], axis=0
            )
            acc_ref[h, :, here] += jnp.dot(left, right, preferred_element_type=F32)
        return carry

    low = jnp.where(c == 1, mate_total, 0.0)
    chip_pre, y_running = prefixes(chip_totals, y)
    middle, x_running = prefixes(x_totals, x)
    high, _ = prefixes(z_totals, z)
    base = low + y_running
    pres = [jnp.zeros_like(low)] + [low + v for v in chip_pre]
    pres += [base + v for v in middle] + [base + x_running + v for v in high]

    def scale(level):
        wide_pre = jnp.concatenate([pres[level][:heads]] * chunks, axis=1)
        return w_ref[1 + local + level] * jnp.exp(cum_ref[...] + wide_pre)

    for level in range(first_z):
        u_s[1 + local + level] = scale(level)
    for bit in range(bz):
        u_s[1 + local + first_z + bit] = jnp.zeros((heads, tokens), F32)
    for bit in range(bz):

        @pl.when(has(z, bit))
        def _():
            u_s[1 + local + first_z + slot_of[bit]] = scale(first_z + bit)

    def z_rights(h, carry):
        one = pl.ds(h, 1)
        for slot in range(bz):
            row = u_s[1 + local + first_z + slot, one, :]
            right_ref[h, slot * 128 : (slot + 1) * 128, :] = (qt_ref[...] * row).astype(BF16)
        return carry

    def level_products(levels):
        def body(h, carry):
            one = pl.ds(h, 1)
            left = jnp.concatenate([lev[level, lax.rem(h, 2), h // 2].astype(BF16) for level in levels], axis=1)
            scales = [u_s[1 + local + level, one, :] for level in levels]
            for i in range(spans):
                here = slice(i * SPAN, (i + 1) * SPAN)
                right = jnp.concatenate([(qt_ref[:, here] * row[:, here]).astype(BF16) for row in scales], axis=0)
                acc_ref[h, :, here] += jnp.dot(left, right, preferred_element_type=F32)
            return carry

        lax.fori_loop(0, heads, body, 0)

    lax.fori_loop(0, heads, z_rights, 0)
    lax.fori_loop(0, heads, local_levels, 0)
    for bit in range(by):

        @pl.when(has(y, bit))
        def _():
            forwarded(1 + bit, 1, bit).wait_recv()

    @pl.when(c == 1)
    def _():
        level0.wait_recv()

    level_products(range(first_x))

    for bit in range(bx):

        @pl.when(has(x, bit))
        def _():
            for oy in range(1 if bit == 0 else 0, ny):
                x_arrived(bit, oy)
            forward(first_x + bit, 1, by + bit).start()

    for count in range(1, bz + 1):

        @pl.when(held == count)
        def _():
            for ox in near:
                for oy in range(ny):
                    if ox or oy:
                        block = z_block(count, lax.rem(y + ny - oy, ny), lax.rem(x + nx - ox, nx))
                        copy(block, block, z_sem, ox * ny + oy, n, wide).wait_recv()
                z_forward(count, c, ox).start()

    for bit in range(bx):

        @pl.when(has(x, bit))
        def _():
            forwarded(first_x + bit, 1, by + bit).wait_recv()

    level_products(range(first_x, first_z))

    swap.wait_send()

    @pl.when(c == 0)
    def _():
        level0.wait_send()

    for o in range(1, ny):
        p1(o).wait_send()
    for o in range(1, nx):
        p2(o).wait_send()
    for o in range(1, nz):

        @pl.when(z + o < nz)
        def _():
            p3(o).wait_send()

    for bit in range(bx):

        @pl.when(has(x, bit))
        def _():
            forward(first_x + bit, 1, by + bit).wait_send()

    @pl.when(jnp.logical_not(has(x, 0)))
    def _():
        for oy in range(ny):
            x_send(0, gbuf, oy, x + 1).wait_send()

    if bx > 1:

        @pl.when(x == 1)
        def _():
            to_row_before().wait_send()
            for oy in range(ny):
                x_send(1, gx.at[1], oy, 2).wait_send()

        @pl.when(x == 0)
        def _():
            for oy in range(ny):
                x_send(1, gx.at[1], oy, 3).wait_send()

    for bit in range(by):
        for o in range(1, ny):

            @pl.when(has(lax.rem(y + o, ny), bit))
            def _():
                y_copy(bit, o).wait_send()

        @pl.when(has(y, bit))
        def _():
            forward(1 + bit, 1, bit).wait_send()

    for count in range(1, bz + 1):

        @pl.when(held == count)
        def _():
            for ox, oy in others:
                z_copy(count, ox, oy).wait_send()
            for ox in near:
                z_forward(count, 1 - c, ox).wait_recv()
            for ox in near:
                z_forward(count, c, ox).wait_send()

    for slot in range(bz):
        for h in range(heads):
            lev_ref[h, :, slot * 128 : (slot + 1) * 128] = lev[first_z + slot, h % 2, h // 2].astype(BF16)


def main_part(ny, nx, nz, queries, keys, values, log_decay, level_weight, gain):
    heads, tokens = log_decay.shape
    by, bx, bz = bits_of(ny), bits_of(nx), bits_of(nz)
    levels = 1 + by + bx + bz
    chunks, spans = tokens // CHUNK, tokens // SPAN
    part = 128 // nx
    dma = pltpu.SemaphoreType.DMA
    return pl.pallas_call(
        functools.partial(main_kernel, ny, nx, nz),
        out_shape=(
            jax.ShapeDtypeStruct((heads, 128, tokens), F32),
            jax.ShapeDtypeStruct((heads, 128, bz * 128), BF16),
            jax.ShapeDtypeStruct((heads, bz * 128, tokens), BF16),
            jax.ShapeDtypeStruct(gain.shape, F32),
        ),
        in_specs=[pl.BlockSpec(memory_space=pltpu.HBM)] * 6,
        out_specs=(VMEM,) * 4,
        scratch_shapes=[
            pltpu.VMEM((2, ny, 136, 128), F32),
            pltpu.VMEM((ny, 136, 128), F32),
            pltpu.VMEM((ny, 136, 128), F32),
            pltpu.VMEM((ny, 136, 128), F32),
            pltpu.VMEM((nx, part + 8, 128), F32),
            pltpu.VMEM((nx, part + 8, 128), F32),
            pltpu.VMEM((128, 128), F32),
            pltpu.VMEM((2, 128, 128), F32),
            pltpu.VMEM((part + 8, 128), F32),
            pltpu.VMEM((nz, part + 8, 128), F32),
            pltpu.VMEM((levels, 2, ny, 128, 128), F32),
            pltpu.VMEM((ny, 128, 128), F32),
            pltpu.VMEM((bz, part, 128), F32),
            pltpu.VMEM((chunks, CHUNK, 2 * CHUNK), BF16),
            pltpu.VMEM((spans, heads, 128, 128), F32),
            pltpu.VMEM((spans, heads, 128, 128), F32),
            pltpu.VMEM((4, heads, tokens), F32),
            pltpu.VMEM((1 + bits_of(spans) + levels, heads, tokens), F32),
            pltpu.VMEM((heads, tokens), F32),
            pltpu.VMEM((128, tokens), F32),
            pltpu.VMEM((heads, tokens), F32),
            dma((2, 1)),
            dma((2, 1)),
            dma((2, ny)),
            dma((2, nx)),
            dma((2, 1)),
            dma((2, nz)),
            dma((2, by * ny)),
            dma((2, bx * ny)),
            dma((2, nx * ny)),
            dma((2, by + bx + nx)),
            dma((6,)),
            pltpu.VMEM(queries.shape, queries.dtype),
            pltpu.VMEM(keys.shape, keys.dtype),
            pltpu.VMEM(values.shape, values.dtype),
            pltpu.VMEM(log_decay.shape, log_decay.dtype),
            pltpu.VMEM(level_weight.shape, level_weight.dtype),
        ],
        compiler_params=pltpu.CompilerParams(collective_id=0, has_side_effects=True, vmem_limit_bytes=40 * 2**20),
    )(*[pltpu.with_memory_space_constraint(v, pltpu.HBM) for v in (queries, keys, values, log_decay, level_weight, gain)])


def finish_kernel(acc_ref, lev_ref, right_ref, gain_ref, out_hbm, out_s, sems):
    heads, _, tokens = acc_ref.shape
    gain = gain_ref[...]
    sends = []
    for i in range(tokens // SPAN):
        at = slice(i * SPAN, (i + 1) * SPAN)
        for h in range(heads):
            mixed = acc_ref[h, :, at] + jnp.dot(lev_ref[h], right_ref[h, :, at], preferred_element_type=F32)
            square = jnp.mean(mixed * mixed, axis=0, keepdims=True)
            normed = (mixed * lax.rsqrt(square + 1e-05)).T
            out_s[at, h * 128 : (h + 1) * 128] = (normed * gain[:, h * 128 : (h + 1) * 128]).astype(BF16)
        send = pltpu.make_async_copy(out_s.at[at], out_hbm.at[at], sems.at[i])
        send.start()
        sends.append(send)
    for send in sends:
        send.wait()


def finish_part(acc, lev, right, gain):
    heads, _, tokens = acc.shape
    return pl.pallas_call(
        finish_kernel,
        out_shape=jax.ShapeDtypeStruct((tokens, heads * 128), BF16),
        in_specs=[VMEM] * 4,
        out_specs=pl.BlockSpec(memory_space=pl.ANY),
        scratch_shapes=[
            pltpu.VMEM((tokens, heads * 128), BF16),
            pltpu.SemaphoreType.DMA((tokens // SPAN,)),
        ],
        compiler_params=pltpu.CompilerParams(vmem_limit_bytes=24 * 2**20),
    )(acc, lev, right, gain)


def per_device(sizes, queries, keys, values, log_decay, level_weight, norm_gain):
    ny, nx, nz = sizes
    gain = norm_gain.reshape(1, -1)
    return finish_part(*main_part(ny, nx, nz, queries, keys, values, log_decay, level_weight, gain))


def solution(mesh, nx=4):
    sizes = (mesh.shape["narrow"] // 2, nx, mesh.shape["wide"] // nx)
    placed = (
        P(("wide", "narrow"), None),
        P(("wide", "narrow"), None),
        P(("wide", "narrow"), None),
        P(None, ("wide", "narrow")),
        P(None, None, ("wide", "narrow")),
        P(),
    )
    return jax.shard_map(
        functools.partial(per_device, sizes),
        mesh=mesh,
        in_specs=placed,
        out_specs=P(("wide", "narrow"), None),
        check_vma=False,
    )
```
